512 devices in a mesh: src: 16 (over y, z_hi), clip: 32 (over z_lo, x, core).
Axes of the slice: x: 4, y: 8, z: 8 (z_hi: 2, z_lo: 4; z = z_hi * 4 + z_lo), core: 2. Of those that a mesh axis runs over, the one named last changes fastest.
Arguments:
- color_masks: float32 [32, 2, 256, 256], P('clip', None, 'src'), may hold values from -1 to 1
- source_weights: float32 [16], P('src'), may hold values from 0.25 to 4
- pupil_shifts: int32 [16, 2], P('src'), may hold values from 0 to 16
- pupils: float32 [8, 2, 32, 32], replicated, may hold values from -6 to 6
- target_labels: int32 [32, 256, 256], P('clip'), may hold values from 0 to 2, as said below
Outputs:
- mask_grad: float32 [32, 2, 256, 256], P('clip', None, 'src')
- source_grad: float32 [16], P('src')
The draws below stay inside these ranges and needn't reach their ends.
Inputs may be any that keep to these rules, and one draw needn't show every extreme that they name: `target_labels`: 0 marks an uncovered pixel, 1 and 2 the pixels of polygons of the first and of the second color.
All inputs are finite; a program needn't handle non-finite values.
Results may differ from the reference program's by a relative error of at most 0.0003.
Values sent between devices are 32-bit elements; how exact they have to be, the bound alone decides.
No kernel may reach another device: no remote copies, remote signals or barrier semaphores. Data moves between devices by JAX's collectives and lax.ppermute only.
A program may use at most 64 MiB of HBM per device.

```python
import math
import jax
import jax.numpy as jnp
from jax import lax

H = 256
K = 48
KP = 32
C = 8
SRC = 16
CLIPS = 32


def draw_target_labels(key, part):
    cover_key, color_key = jax.random.split(key)
    clip_ids = jnp.arange(CLIPS, dtype=jnp.int32)[:, None, None]
    cover_limit = 100 + 900 * clip_ids // max(CLIPS - 1, 1)
    cover_draw = jax.random.randint(cover_key, (CLIPS, H, H), 0, 1000)
    color_ids = jax.random.randint(color_key, (CLIPS, H, H), 1, 3)
    return jnp.where(cover_draw < cover_limit, color_ids, 0).astype(jnp.int32)


def touch_ends(entries, key, smallest, largest):
    longest = entries.shape.index(max(entries.shape))
    spots = []
    for shift in (0, 1):
        where = [jax.random.randint(jax.random.fold_in(key, axis), (), 0, length) for axis, length in enumerate(entries.shape)]
        where[longest] = (where[longest] + shift) % entries.shape[longest]
        spots.append(tuple(where))
    return entries.at[spots[0]].set(smallest).at[spots[1]].set(largest)


def level_of(own_key, dims, cuts, low, largest):
    loudness, own = 1.0, jax.random.fold_in(own_key, 6)
    for position, parts in cuts:
        steps = jnp.exp(jax.random.uniform(jax.random.fold_in(own, position), (parts,), jnp.float32, low / len(cuts), largest / len(cuts)))
        loudness = loudness * jnp.repeat(steps, dims[position] // parts).reshape([-1 if axis == position else 1 for axis in range(len(dims))])
    return loudness


def scatter_about(stream_key, extent, deviation, bound, kind=jnp.bfloat16):
    return jnp.clip(deviation * jax.random.normal(stream_key, extent, jnp.float32), -bound, bound).astype(kind)


def setup_inputs(seed: int = 0) -> dict:
    splits = jax.random.split(jax.random.key(seed), 6)
    color_masks = jnp.clip(jax.random.uniform(splits[0], (CLIPS, 2, H, H), jnp.float32, -1.0, 1.0) * level_of(splits[0], (CLIPS, 2, H, H), ((0, 32), (2, 16)), -0.4, 0.0), -1.0, 1.0)
    source_weights = jnp.clip(jnp.exp(math.log(4.0) - 2.7725887 * jax.random.uniform(splits[1], (SRC,), jnp.float32) ** level_of(splits[1], (SRC,), ((0, 16),), -0.2, 0.2)), 0.25, 4.0)
    pupil_shifts = touch_ends(jax.random.randint(splits[2], (SRC, 2), 0, K - KP + 1), jax.random.fold_in(splits[2], 1), 0, K - KP).astype(jnp.int32)
    pupils = scatter_about(splits[3], (C, 2, KP, KP), 1.0, 6.0, jnp.float32)
    target_labels = draw_target_labels(jax.random.fold_in(splits[5], 71), 0)
    return dict(color_masks=color_masks, source_weights=source_weights, pupil_shifts=pupil_shifts, pupils=pupils, target_labels=target_labels)


steepness = 4.0
threshold = 0.6
loss_weight = 2.0
binarize = 0.25
highest = lax.Precision.HIGHEST

def make_tables(height, band_size, pupil_size):
    pixels = jnp.arange(height, dtype=jnp.int32)
    frequency = jnp.arange(band_size, dtype=jnp.int32) - band_size // 2
    phases = frequency[:, None] * pixels[None, :] % height
    angles = phases.astype(jnp.float32) * (2.0 * math.pi / height)
    scaling = 1.0 / math.sqrt(height * pupil_size)
    forward_cos = jnp.cos(angles) * scaling
    forward_sin = -jnp.sin(angles) * scaling
    pupil_freq = jnp.arange(pupil_size, dtype=jnp.int32) - pupil_size // 2
    back_phases = pixels[:, None] * pupil_freq[None, :] % height
    back_angles = back_phases.astype(jnp.float32) * (2.0 * math.pi / height)
    return (forward_cos, forward_sin, jnp.cos(back_angles), jnp.sin(back_angles))

def matmul(left, right):
    return jnp.dot(left, right, precision=highest, preferred_element_type=jnp.float32)

def contract(form, left, right):
    return jnp.einsum(form, left, right, precision=highest, preferred_element_type=jnp.float32)

def spectrum(field_rows, row_cos, row_sin, col_cos, col_sin):
    cos_part = matmul(field_rows, col_cos.T)
    sin_part = matmul(field_rows, col_sin.T)
    real_part = matmul(row_cos, cos_part) - matmul(row_sin, sin_part)
    imag_part = matmul(row_cos, sin_part) + matmul(row_sin, cos_part)
    return (real_part, imag_part)

def pupil_image(win_real, win_imag, pupils, inverse_cos, inverse_sin):
    pupil_real = pupils[:, 0]
    pupil_imag = pupils[:, 1]
    product_real = pupil_real * win_real[None] - pupil_imag * win_imag[None]
    product_imag = pupil_real * win_imag[None] + pupil_imag * win_real[None]
    half_real = contract('cij,yj->ciy', product_real, inverse_cos) - contract('cij,yj->ciy', product_imag, inverse_sin)
    half_imag = contract('cij,yj->ciy', product_real, inverse_sin) + contract('cij,yj->ciy', product_imag, inverse_cos)
    return (half_real, half_imag)

def field_power(half_real, half_imag, row_cos, row_sin):
    field_real = contract('xi,ciy->cxy', row_cos, half_real) - contract('xi,ciy->cxy', row_sin, half_imag)
    field_imag = contract('xi,ciy->cxy', row_cos, half_imag) + contract('xi,ciy->cxy', row_sin, half_real)
    return lax.optimization_barrier(jnp.sum(field_real * field_real + field_imag * field_imag, axis=0))

def clip_loss(masks_here, source_weights, pupil_shifts, pupils, labels, tables):
    forward_cos, forward_sin, inverse_cos, inverse_sin = tables
    source_count = source_weights.shape[0]
    channels = pupils.shape[0]
    total_loss = jnp.zeros((), jnp.float32)
    for color in range(2):
        spec_real, spec_imag = spectrum(masks_here[color], forward_cos, forward_sin, forward_cos, forward_sin)

        def add_source(summed, inputs):
            weight, shift = inputs
            first = shift[0].astype(jnp.int32)
            second = shift[1].astype(jnp.int32)
            win_real = lax.dynamic_slice(spec_real, (first, second), (KP, KP))
            win_imag = lax.dynamic_slice(spec_imag, (first, second), (KP, KP))
            half_real, half_imag = pupil_image(win_real, win_imag, pupils, inverse_cos, inverse_sin)
            power = field_power(half_real, half_imag, inverse_cos, inverse_sin)
            return (summed + weight * power / (channels * source_count), None)
        intensity, _ = lax.scan(add_source, jnp.zeros((H, H), jnp.float32), (source_weights, pupil_shifts))
        resist = jax.nn.sigmoid(steepness * (intensity - threshold))
        goal = (labels == color + 1).astype(jnp.float32)
        plane = masks_here[color]
        total_loss = total_loss + loss_weight * jnp.sum((resist - goal) ** 2) + binarize * jnp.sum((1.0 - plane * plane) ** 2)
    return total_loss

def reference(color_masks, source_weights, pupil_shifts, pupils, target_labels):
    tables = make_tables(H, K, KP)
    grad_fn = jax.grad(clip_loss, argnums=(0, 1))

    def one_clip(inputs):
        masks_here, labels = inputs
        return grad_fn(masks_here, source_weights, pupil_shifts, pupils, labels, tables)
    mask_grad, weight_grads = lax.map(one_clip, (color_masks, target_labels))
    source_grad = lax.optimization_barrier(jnp.sum(weight_grads, axis=0)) * (SRC / (2.0 * CLIPS * H * H))
    return (mask_grad, source_grad)
```

```python
import math

import jax
import jax.numpy as jnp
import numpy as np
import ml_dtypes
from jax import lax
from jax.experimental import pallas as pl
from jax.experimental.pallas import tpu as pltpu
from jax.sharding import PartitionSpec as P

H = 256
K = 48
KP = 32
C = 8
SRC = 16
CLIPS = 32
N = 64
ROWS = 16

steepness = 4.0
threshold = 0.6
loss_weight = 2.0
binarize = 0.25
f32 = jnp.float32
bf16 = jnp.bfloat16

LANE_WEIGHT, LANE_A, LANE_B, LANE_DEST = 56, 57, 58, 59


def np_split(a):
    a = np.asarray(a, np.float64)
    hi = a.astype(ml_dtypes.bfloat16)
    lo = (a - hi.astype(np.float64)).astype(ml_dtypes.bfloat16)
    return hi, lo


def tables():
    scale = 1.0 / math.sqrt(H * KP)
    x = np.arange(H)
    f = np.arange(K) - K // 2
    ang = 2 * np.pi * ((f[:, None] * x[None, :]) % H) / H
    fc, fs = np.cos(ang) * scale, -np.sin(ang) * scale
    t = {}
    col = np.zeros((2 * H, 128))
    for k in range(2):
        for p in range(25):
            a = 2 * np.pi * ((p * x) % H) / H
            col[k * H : (k + 1) * H, 64 * k + p] = np.cos(a) * scale
            if p:
                col[k * H : (k + 1) * H, 64 * k + 24 + p] = -np.sin(a) * scale
    hi, lo = np_split(col)
    t["col"] = np.concatenate([hi, lo], 1)
    hi, lo = np_split(np.concatenate([fc, fs], 0))
    t["row"] = np.concatenate([hi, lo], 0)
    ex = np.zeros((256, 256))
    for k in range(2):
        for g in range(K):
            p = g - K // 2
            q, s = abs(p), np.sign(p)
            re, im = 128 * k + g, 128 * k + 64 + g
            ex[64 * k + q, re] += 1
            ex[128 + 64 * k + q, im] += 1
            if q:
                ex[128 + 64 * k + 24 + q, re] -= s
                ex[64 * k + 24 + q, im] += s
    t["ex"] = ex.astype(ml_dtypes.bfloat16)
    u = np.arange(N)
    i = np.arange(KP) - KP // 2
    a = 2 * np.pi * ((u[:, None] * i[None, :]) % N) / N
    br, bi = np.cos(a), np.sin(a)
    g1 = np.zeros((128, 256))
    for k in range(2):
        r, m = slice(64 * k, 64 * k + 32), slice(64 * k + 32, 64 * k + 64)
        o, q = slice(64 * k, 64 * k + 64), slice(128 + 64 * k, 128 + 64 * k + 64)
        g1[r, o] = br.T
        g1[m, o] = -bi.T
        g1[r, q] = bi.T
        g1[m, q] = br.T
    hi, lo = np_split(g1)
    t["g1"] = np.concatenate([hi, hi, lo], 0)
    t["g1t"] = np.concatenate([hi.T, lo.T], 1)
    d2 = np.block([[br, -bi], [bi, br]])
    hi, lo = np_split(d2)
    t["d2"] = np.concatenate([hi, hi, lo], 1)
    z = np.zeros_like(lo.T)
    t["d2t"] = np.concatenate(
        [np.concatenate([hi.T, hi.T], 1), np.concatenate([lo.T, z], 1)], 0
    )
    fr = np.arange(-31, 32)
    dx = x[:, None] / H - u[None, :] / N
    up = np.cos(2 * np.pi * fr[:, None, None] * dx[None]).sum(0) / N
    hi, lo = np_split(up)
    t["up"] = np.concatenate([hi, hi, lo], 1)
    t["upt"] = np.concatenate([hi.T, lo.T], 0)
    v = np.zeros((128, 512))
    v[:64, :256] = up.T
    v[64:, 256:] = up.T
    hi, lo = np_split(v)
    t["v"] = np.concatenate([hi, hi, lo], 0)
    t["vt"] = np.concatenate([hi.T, lo.T], 1)
    loc = np.zeros((SRC, 2 * ROWS, K))
    for d in range(SRC):
        sl = slice(ROWS * d, ROWS * d + ROWS)
        loc[d, :ROWS] = fc[:, sl].T
        loc[d, ROWS:] = fs[:, sl].T
    hi, lo = np_split(loc)
    t["loc"] = np.concatenate(
        [hi, lo, np.zeros((SRC, 2 * ROWS, 32), ml_dtypes.bfloat16)], 2
    )
    fin = np.zeros((256, 256))
    fin[0:48] = fc
    fin[64:112] = fs
    fin[128:176] = -fs
    fin[192:240] = fc
    hi, lo = np_split(fin)
    t["fin"] = np.concatenate([hi, lo], 1)
    return t


T = tables()


def split(x):
    hi = x.astype(bf16)
    lo = (x - hi.astype(f32)).astype(bf16)
    return hi, lo


def dot(a, b):
    return lax.dot_general(
        a, b, (((1,), (0,)), ((), ())), preferred_element_type=f32
    )


def lane_of(shape):
    return lax.broadcasted_iota(jnp.int32, shape, len(shape) - 1)


def send_kernel(mask_ref, weight_ref, shift_ref, col_ref, out_ref):
    m = jnp.concatenate([mask_ref[0, 0], mask_ref[0, 1]], axis=1)
    hi, lo = split(m)
    r = dot(jnp.concatenate([hi, lo], 0), col_ref[...])
    rows = r[:16, :128] + r[16:, :128] + r[:16, 128:]
    lane = lane_of((16, 128))
    rows = jnp.where(lane == LANE_WEIGHT, weight_ref[0], rows)
    rows = jnp.where(lane == LANE_A, shift_ref[0, 0].astype(f32), rows)
    rows = jnp.where(lane == LANE_B, shift_ref[0, 1].astype(f32), rows)
    for d in range(SRC):
        out_ref[d] = jnp.where(lane == LANE_DEST, float(d), rows)


def pupil_kernel(pupil_ref, pr_ref, pi_ref):
    lane = lane_of((KP, 128))
    sign = jnp.where((lane // 32) % 2 == 0, -1.0, 1.0)
    for c in range(C):
        re, im = pupil_ref[c, 0], pupil_ref[c, 1]
        pr_ref[c] = jnp.concatenate([re] * 4, axis=1)
        pi_ref[c] = jnp.concatenate([im] * 4, axis=1) * sign


def scalars(g_ref, s):
    row = g_ref[s, 0:1, :]
    lane = lane_of((1, 128))

    def pick(which):
        return jnp.sum(jnp.where(lane == which, row, 0.0))

    a = jnp.clip(pick(LANE_A).astype(jnp.int32), 0, K - KP)
    b = jnp.clip(pick(LANE_B).astype(jnp.int32), 0, K - KP)
    return pick(LANE_WEIGHT), a, b


def forward_kernel(
    g_ref, pr_ref, pi_ref, label_ref, row_ref, ex_ref, g1_ref, d2_ref, up_ref, upt_ref,
    v_ref, vt_ref, fld_ref, grad_ref, dw_ref, spec_ref, pw_ref,
):
    g = g_ref[...].reshape(H, 128)
    hi, lo = split(g)
    r = dot(row_ref[...], hi)
    u = r[:96] + r[96:] + dot(row_ref[:96, :], lo)
    uu = jnp.concatenate([u[:48], u[48:]], axis=1)
    hi, lo = split(uu)
    r = dot(jnp.concatenate([hi, lo], 0), ex_ref[...])
    r = r[:48] + r[48:]
    spec_ref[0] = r[:, :128]
    spec_ref[1] = r[:, 128:]
    lane = lane_of((KP, 128))
    block = lane // 32

    def source(s, total):
        w, a, b = scalars(g_ref, s)
        w0 = spec_ref[0, pl.ds(a, KP), :]
        w1 = spec_ref[1, pl.ds(a, KP), :]
        win = jnp.where(
            block < 2,
            jnp.where(block == 0, pltpu.roll(w0, 128 - b, 1), pltpu.roll(w0, 96 - b, 1)),
            jnp.where(block == 2, pltpu.roll(w1, 64 - b, 1), pltpu.roll(w1, 32 - b, 1)),
        )
        swp = jnp.where(block % 2 == 0, pltpu.roll(win, 96, 1), pltpu.roll(win, 32, 1))
        his, los = [], []
        for c in range(C):
            h, l = split(win * pr_ref[c] + swp * pi_ref[c])
            his.append(h)
            los.append(l)
        xhi, xlo = jnp.concatenate(his, 0), jnp.concatenate(los, 0)
        t = dot(jnp.concatenate([xhi, xlo], 1), g1_ref[0:256, :]) + dot(
            xhi, g1_ref[256:384, :]
        )
        thi, tlo = split(t)
        pw = jnp.zeros((N, 128), f32)
        for p in range(C // 2):
            halves = []
            for c in (2 * p, 2 * p + 1):
                rs = slice(KP * c, KP * c + KP)
                halves.append(
                    jnp.concatenate(
                        [thi[rs, :128], thi[rs, 128:], tlo[rs, :128], tlo[rs, 128:],
                         thi[rs, :128], thi[rs, 128:]], 0)
                )
            fld = dot(d2_ref[...], jnp.concatenate(halves, 1))
            fld_ref[s, p] = fld
            q = fld * fld
            q = q[:N] + q[N:]
            pw = pw + (q[:, :128] + q[:, 128:])
        pw_ref[s] = pw
        return total + w * pw

    total = lax.fori_loop(0, SRC, source, jnp.zeros((N, 128), f32))
    hi, lo = split(total * (1.0 / (C * SRC)))
    y = dot(up_ref[...], jnp.concatenate([hi, lo, hi], 0))
    hi, lo = split(y)
    intensity = dot(jnp.concatenate([hi, lo], 1), v_ref[0:256, :]) + dot(hi, v_ref[256:384, :])
    resist = 1.0 / (1.0 + jnp.exp(-steepness * (intensity - threshold)))
    labels = label_ref[0]
    goal = jnp.concatenate(
        [(labels == 1).astype(f32), (labels == 2).astype(f32)], axis=1
    )
    lg = (loss_weight * 2.0 * steepness) * (resist - goal) * resist * (1.0 - resist)
    hi, lo = split(lg)
    r = dot(hi, vt_ref[...])
    z = r[:, :128] + r[:, 128:] + dot(lo, vt_ref[:, :128])
    hi, lo = split(z)
    r = dot(upt_ref[...], hi)
    lgrad = r[:N] + r[N:] + dot(upt_ref[:N, :], lo)
    grad_ref[...] = lgrad
    row = g_ref[0, 0:1, :]
    own = jnp.sum(jnp.where(lane_of((1, 128)) == LANE_DEST, row, 0.0)).astype(jnp.int32)
    own = jnp.clip(own, 0, SRC - 1)
    part = jnp.sum(pw_ref[own] * lgrad, axis=0, keepdims=True)
    part = part * (SRC / (2.0 * CLIPS * H * H) / (C * SRC))
    dw_ref[...] = jnp.broadcast_to(part, (CLIPS, 128))


def backward_kernel(
    g_ref, fld_ref, grad_ref, pr_ref, pi_ref, mask_ref, d2t_ref, g1t_ref, loc_ref, fin_ref,
    out_ref, acc_ref,
):
    acc_ref[...] = jnp.zeros_like(acc_ref)
    lg = grad_ref[...]
    lg = jnp.concatenate([lg, lg], 0)
    lg = jnp.concatenate([lg, lg], 1)
    lane = lane_of((KP, 128))
    block = lane // 32

    def source(s, carry):
        w, a, b = scalars(g_ref, s)
        his, los = [], []
        for p in range(C // 2):
            hi, lo = split(fld_ref[s, p] * lg)
            r = dot(d2t_ref[...], jnp.concatenate([hi, lo], 0))
            dt = r[:64] + r[64:]
            for h in range(2):
                one = dt[:, 128 * h : 128 * h + 128]
                hi, lo = split(jnp.concatenate([one[:32], one[32:]], 1))
                his.append(hi)
                los.append(lo)
        r = dot(jnp.concatenate(his, 0), g1t_ref[...])
        dx = r[:, :128] + r[:, 128:] + dot(jnp.concatenate(los, 0), g1t_ref[:, :128])
        same = jnp.zeros((KP, 128), f32)
        cross = jnp.zeros((KP, 128), f32)
        for c in range(C):
            one = dx[KP * c : KP * c + KP]
            same = same + one * pr_ref[c]
            cross = cross + one * pi_ref[c]
        dwin = same + jnp.where(
            block % 2 == 0, pltpu.roll(cross, 96, 1), pltpu.roll(cross, 32, 1)
        )
        dwin = dwin * (w * (2.0 / (C * SRC)))
        pieces = [jnp.where(block == q, dwin, 0.0) for q in range(4)]
        k0 = pltpu.roll(pieces[0], b, 1) + pltpu.roll(pieces[1], 32 + b, 1)
        k1 = pltpu.roll(pieces[2], 64 + b, 1) + pltpu.roll(pieces[3], 96 + b, 1)
        acc_ref[0, pl.ds(a, KP), :] += k0
        acc_ref[1, pl.ds(a, KP), :] += k1
        return carry

    lax.fori_loop(0, SRC, source, 0)
    row = g_ref[0, 0:1, :]
    own = jnp.sum(jnp.where(lane_of((1, 128)) == LANE_DEST, row, 0.0)).astype(jnp.int32)
    own = jnp.clip(own, 0, SRC - 1)
    loc = loc_ref[own]
    lhi, llo = loc[:, :48], loc[:, 48:96]
    hi, lo = split(jnp.concatenate([acc_ref[0], acc_ref[1]], 1))
    q = dot(lhi, hi) + dot(llo, hi) + dot(lhi, lo)
    both = []
    for k in range(2):
        ks = slice(128 * k, 128 * k + 128)
        both.append(jnp.concatenate([q[:16, ks], q[16:, ks]], 1))
    q = jnp.concatenate(both, 0)
    hi, lo = split(q)
    r = dot(hi, fin_ref[...])
    dm = r[:, :256] + r[:, 256:] + dot(lo, fin_ref[:, :256])
    for k in range(2):
        m = mask_ref[0, k]
        out_ref[0, k] = dm[16 * k : 16 * k + 16] - (4.0 * binarize) * m * (1.0 - m * m)


def spec(space=pltpu.VMEM):
    return pl.BlockSpec(memory_space=space)


def const(name):
    return jnp.asarray(T[name])


params = pltpu.CompilerParams(vmem_limit_bytes=50 * 1024 * 1024)


def send(masks, weights, shifts):
    return pl.pallas_call(
        send_kernel,
        out_shape=jax.ShapeDtypeStruct((SRC, ROWS, 128), f32),
        in_specs=[spec(), spec(pltpu.SMEM), spec(pltpu.SMEM), spec()],
        out_specs=spec(),
        name="send",
    )(masks, weights, shifts, const("col"))


def pupil_lanes(pupils):
    shape = jax.ShapeDtypeStruct((C, KP, 128), f32)
    return pl.pallas_call(
        pupil_kernel, out_shape=(shape, shape), in_specs=[spec()], out_specs=(spec(), spec()),
        name="pupil_lanes",
    )(pupils)


def forward(gathered, pr, pi, labels):
    names = ("row", "ex", "g1", "d2", "up", "upt", "v", "vt")
    return pl.pallas_call(
        forward_kernel,
        out_shape=(
            jax.ShapeDtypeStruct((SRC, C // 2, 128, 256), f32),
            jax.ShapeDtypeStruct((N, 128), f32),
            jax.ShapeDtypeStruct((CLIPS, 128), f32),
        ),
        in_specs=[spec()] * (4 + len(names)),
        out_specs=(spec(), spec(), spec()),
        scratch_shapes=[pltpu.VMEM((2, K, 128), f32), pltpu.VMEM((SRC, N, 128), f32)],
        compiler_params=params,
        name="forward",
    )(gathered, pr, pi, labels, *[const(n) for n in names])


def backward(gathered, fld, grad, pr, pi, masks):
    names = ("d2t", "g1t", "loc", "fin")
    return pl.pallas_call(
        backward_kernel,
        out_shape=jax.ShapeDtypeStruct((1, 2, ROWS, H), f32),
        in_specs=[spec()] * (6 + len(names)),
        out_specs=spec(),
        scratch_shapes=[pltpu.VMEM((2, K, 128), f32)],
        compiler_params=params,
        name="backward",
    )(gathered, fld, grad, pr, pi, masks, *[const(n) for n in names])


def per_device(color_masks, source_weights, pupil_shifts, pupils, target_labels):
    rows = send(color_masks, source_weights, pupil_shifts)
    gathered = lax.all_to_all(rows, "src", 0, 0, tiled=True)
    pr, pi = pupil_lanes(pupils)
    fld, grad, dw = forward(gathered, pr, pi, target_labels)
    parts = lax.all_to_all(dw, "clip", 0, 0, tiled=True)
    mask_grad = backward(gathered, fld, grad, pr, pi, color_masks)
    return mask_grad, jnp.sum(parts)[None]


def solution(mesh):
    in_specs = (P("clip", None, "src", None), P("src"), P("src", None), P(), P("clip", None, None))
    out_specs = (P("clip", None, "src", None), P("src"))
    return jax.shard_map(
        per_device, mesh=mesh, in_specs=in_specs, out_specs=out_specs, check_vma=False
    )
```

```python
import math

import jax
import jax.numpy as jnp
import numpy as np
import ml_dtypes
from jax import lax
from jax.experimental import pallas as pl
from jax.experimental.pallas import tpu as pltpu
from jax.sharding import PartitionSpec as P

H = 256
K = 48
KP = 32
C = 8
SRC = 16
CLIPS = 32
N = 64
ROWS = 16

steepness = 4.0
threshold = 0.6
loss_weight = 2.0
binarize = 0.25
f32 = jnp.float32
bf16 = jnp.bfloat16

LANE_WEIGHT, LANE_A, LANE_B, LANE_DEST = 56, 57, 58, 59


def np_split(a):
    a = np.asarray(a, np.float64)
    hi = a.astype(ml_dtypes.bfloat16)
    lo = (a - hi.astype(np.float64)).astype(ml_dtypes.bfloat16)
    return hi, lo


def tables():
    scale = 1.0 / math.sqrt(H * KP)
    x = np.arange(H)
    f = np.arange(K) - K // 2
    ang = 2 * np.pi * ((f[:, None] * x[None, :]) % H) / H
    fc, fs = np.cos(ang) * scale, -np.sin(ang) * scale
    t = {}
    col = np.zeros((2 * H, 128))
    for k in range(2):
        for p in range(25):
            a = 2 * np.pi * ((p * x) % H) / H
            col[k * H : (k + 1) * H, 64 * k + p] = np.cos(a) * scale
            if p:
                col[k * H : (k + 1) * H, 64 * k + 24 + p] = -np.sin(a) * scale
    hi, lo = np_split(col)
    t["col"] = np.concatenate([hi, lo], 1)
    hi, lo = np_split(np.concatenate([fc, fs], 0))
    t["row"] = np.concatenate([hi, lo], 0)
    ex = np.zeros((256, 256))
    for k in range(2):
        for g in range(K):
            p = g - K // 2
            q, s = abs(p), np.sign(p)
            re, im = 128 * k + g, 128 * k + 64 + g
            ex[64 * k + q, re] += 1
            ex[128 + 64 * k + q, im] += 1
            if q:
                ex[128 + 64 * k + 24 + q, re] -= s
                ex[64 * k + 24 + q, im] += s
    t["ex"] = ex.astype(ml_dtypes.bfloat16)
    u = np.arange(N)
    i = np.arange(KP) - KP // 2
    a = 2 * np.pi * ((u[:, None] * i[None, :]) % N) / N
    br, bi = np.cos(a), np.sin(a)
    g1 = np.zeros((128, 256))
    for k in range(2):
        r, m = slice(64 * k, 64 * k + 32), slice(64 * k + 32, 64 * k + 64)
        o, q = slice(64 * k, 64 * k + 64), slice(128 + 64 * k, 128 + 64 * k + 64)
        g1[r, o] = br.T
        g1[m, o] = -bi.T
        g1[r, q] = bi.T
        g1[m, q] = br.T
    hi, lo = np_split(g1)
    t["g1"] = np.concatenate([hi, hi, lo], 0)
    t["g1t"] = np.concatenate([hi.T, lo.T], 1)
    d2 = np.block([[br, -bi], [bi, br]])
    hi, lo = np_split(d2)
    t["d2"] = np.concatenate([hi, hi, lo], 1)
    z = np.zeros_like(lo.T)
    t["d2t"] = np.concatenate(
        [np.concatenate([hi.T, hi.T], 1), np.concatenate([lo.T, z], 1)], 0
    )
    fr = np.arange(-31, 32)
    dx = x[:, None] / H - u[None, :] / N
    up = np.cos(2 * np.pi * fr[:, None, None] * dx[None]).sum(0) / N
    hi, lo = np_split(up)
    t["up"] = np.concatenate([hi, hi, lo], 1)
    t["upt"] = np.concatenate([hi.T, lo.T], 0)
    v = np.zeros((128, 512))
    v[:64, :256] = up.T
    v[64:, 256:] = up.T
    hi, lo = np_split(v)
    t["v"] = np.concatenate([hi, hi, lo], 0)
    t["vt"] = np.concatenate([hi.T, lo.T], 1)
    loc = np.zeros((SRC, 2 * ROWS, K))
    for d in range(SRC):
        sl = slice(ROWS * d, ROWS * d + ROWS)
        loc[d, :ROWS] = fc[:, sl].T
        loc[d, ROWS:] = fs[:, sl].T
    hi, lo = np_split(loc)
    t["loc"] = np.concatenate(
        [hi, lo, np.zeros((SRC, 2 * ROWS, 32), ml_dtypes.bfloat16)], 2
    )
    fin = np.zeros((256, 256))
    fin[0:48] = fc
    fin[64:112] = fs
    fin[128:176] = -fs
    fin[192:240] = fc
    hi, lo = np_split(fin)
    t["fin"] = np.concatenate([hi, lo], 1)
    return t


FORWARD = ("row", "ex", "g1", "d2", "up", "upt", "v", "vt")
BACKWARD = ("d2t", "g1t", "fin")


def pack(t, names):
    parts, place, at = [], {}, 0
    for name in names:
        a = t[name]
        if a.shape[1] == 512:
            a = np.concatenate([a[:, :256], a[:, 256:]], 0)
        a = np.pad(a, ((0, 0), (0, 256 - a.shape[1])))
        parts.append(a)
        place[name] = (at, a.shape[0])
        at += a.shape[0]
    return np.concatenate(parts, 0), place


T = tables()
FORWARD_TABLE, FORWARD_PLACE = pack(T, FORWARD)
BACKWARD_TABLE, BACKWARD_PLACE = pack(T, BACKWARD)


def view(ref, place, name, first=0, count=None, lanes=slice(None)):
    at, rows = place[name]
    return ref[at + first : at + (rows if count is None else first + count), lanes]


def split(x):
    hi = x.astype(bf16)
    lo = (x - hi.astype(f32)).astype(bf16)
    return hi, lo


def dot(a, b):
    return lax.dot_general(
        a, b, (((1,), (0,)), ((), ())), preferred_element_type=f32
    )


def lane_of(shape):
    return lax.broadcasted_iota(jnp.int32, shape, len(shape) - 1)


def send_kernel(mask_ref, weight_ref, shift_ref, col_ref, out_ref):
    m = jnp.concatenate([mask_ref[0, 0], mask_ref[0, 1]], axis=1)
    hi, lo = split(m)
    r = dot(jnp.concatenate([hi, lo], 0), col_ref[...])
    rows = r[:16, :128] + r[16:, :128] + r[:16, 128:]
    lane = lane_of((16, 128))
    rows = jnp.where(lane == LANE_WEIGHT, weight_ref[0, 0], rows)
    rows = jnp.where(lane == LANE_A, shift_ref[0, 0].astype(f32), rows)
    rows = jnp.where(lane == LANE_B, shift_ref[0, 1].astype(f32), rows)
    for d in range(SRC):
        out_ref[d] = jnp.where(lane == LANE_DEST, float(d), rows)


def prepare_kernel(pupil_ref, label_ref, tab_ref, pr_ref, pi_ref, goal_ref, out_ref):
    del tab_ref, out_ref
    sign = jnp.where((lane_of((KP, 128)) // 32) % 2 == 0, -1.0, 1.0)
    for c in range(C):
        re, im = pupil_ref[c, 0], pupil_ref[c, 1]
        pr_ref[c] = jnp.concatenate([re] * 4, axis=1)
        pi_ref[c] = jnp.concatenate([im] * 4, axis=1) * sign
    for k in range(2):
        goal_ref[:, H * k : H * k + H] = (label_ref[0] == k + 1).astype(f32)


def picked(row, which):
    return jnp.sum(jnp.where(lane_of((1, 128)) == which, row, 0.0))


def place_of(row, which, largest):
    return jnp.clip(picked(row, which).astype(jnp.int32), 0, largest)


def forward_kernel(g_ref, pr_ref, pi_ref, goal_ref, tab_ref, fld_ref, small_ref, dw_ref, spec_ref, pw_ref):
    def tab(name, *args, **kwargs):
        return view(tab_ref, FORWARD_PLACE, name, *args, **kwargs)

    g = g_ref[...].reshape(H, 128)
    hi, lo = split(g)
    r = dot(tab("row"), hi)
    u = r[:96] + r[96:] + dot(tab("row", 0, 96), lo)
    uu = jnp.concatenate([u[:48], u[48:]], axis=1)
    hi, lo = split(uu)
    r = dot(jnp.concatenate([hi, lo], 0), tab("ex"))
    r = r[:48] + r[48:]
    spec_ref[0] = r[:, :128]
    spec_ref[1] = r[:, 128:]
    block = lane_of((KP, 128)) // 32

    def source(s, total):
        row = g_ref[s, 0:1, :]
        small_ref[N + s : N + s + 1, :] = row
        w = picked(row, LANE_WEIGHT)
        a, b = place_of(row, LANE_A, K - KP), place_of(row, LANE_B, K - KP)
        w0 = spec_ref[0, pl.ds(a, KP), :]
        w1 = spec_ref[1, pl.ds(a, KP), :]
        win = jnp.where(
            block < 2,
            jnp.where(block == 0, pltpu.roll(w0, 128 - b, 1), pltpu.roll(w0, 96 - b, 1)),
            jnp.where(block == 2, pltpu.roll(w1, 64 - b, 1), pltpu.roll(w1, 32 - b, 1)),
        )
        swp = jnp.where(block % 2 == 0, pltpu.roll(win, 96, 1), pltpu.roll(win, 32, 1))
        his, los = [], []
        for c in range(C):
            h, l = split(win * pr_ref[c] + swp * pi_ref[c])
            his.append(h)
            los.append(l)
        xhi, xlo = jnp.concatenate(his, 0), jnp.concatenate(los, 0)
        t = dot(jnp.concatenate([xhi, xlo], 1), tab("g1", 0, 256)) + dot(xhi, tab("g1", 256, 128))
        thi, tlo = split(t)
        pw = jnp.zeros((N, 128), f32)
        for p in range(C // 2):
            halves = []
            for c in (2 * p, 2 * p + 1):
                rs = slice(KP * c, KP * c + KP)
                halves.append(
                    jnp.concatenate(
                        [thi[rs, :128], thi[rs, 128:], tlo[rs, :128], tlo[rs, 128:],
                         thi[rs, :128], thi[rs, 128:]], 0)
                )
            fld = dot(tab("d2", lanes=slice(0, 192)), jnp.concatenate(halves, 1))
            fld_ref[s, p] = fld
            q = fld * fld
            q = q[:N] + q[N:]
            pw = pw + (q[:, :128] + q[:, 128:])
        pw_ref[s] = pw
        return total + w * pw

    total = jnp.zeros((N, 128), f32)
    for s in range(SRC):
        total = source(s, total)
    hi, lo = split(total * (1.0 / (C * SRC)))
    y = dot(tab("up", lanes=slice(0, 192)), jnp.concatenate([hi, lo, hi], 0))
    hi, lo = split(y)
    both = jnp.concatenate([hi, lo], 1)
    z = jnp.zeros((H, 128), f32)
    for k in range(2):
        intensity = dot(both, tab("v", 384 * k, 256)) + dot(hi, tab("v", 384 * k + 256, 128))
        resist = 1.0 / (1.0 + jnp.exp(-steepness * (intensity - threshold)))
        lg = (resist - goal_ref[:, H * k : H * k + H]) * resist * (1.0 - resist)
        ghi, glo = split((loss_weight * 2.0 * steepness) * lg)
        r = dot(ghi, tab("vt", H * k, H))
        z = z + (r[:, :128] + r[:, 128:] + dot(glo, tab("vt", H * k, H, lanes=slice(0, 128))))
    hi, lo = split(z)
    r = dot(tab("upt"), hi)
    lgrad = r[:N] + r[N:] + dot(tab("upt", 0, N), lo)
    small_ref[0:N, :] = lgrad
    own = place_of(g_ref[0, 0:1, :], LANE_DEST, SRC - 1)
    part = jnp.sum(pw_ref[own] * lgrad, axis=0, keepdims=True)
    part = part * (SRC / (2.0 * CLIPS * H * H) / (C * SRC))
    dw_ref[...] = jnp.broadcast_to(part, (CLIPS, 128))


def backward_kernel(
    fld_hbm, small_hbm, pr_hbm, pi_hbm, mask_hbm, tab_hbm, loc_hbm, out_ref,
    fld_ref, small_ref, pr_ref, pi_ref, mask_ref, tab_ref, loc_ref, acc_ref, sems,
):
    copies = [
        pltpu.make_async_copy(src, dst, sems.at[i])
        for i, (src, dst) in enumerate(
            ((small_hbm, small_ref), (tab_hbm, tab_ref), (pr_hbm, pr_ref), (pi_hbm, pi_ref),
             (mask_hbm, mask_ref), (loc_hbm, loc_ref))
        )
    ]
    fields = [
        pltpu.make_async_copy(fld_hbm.at[s], fld_ref.at[s], sems.at[len(copies) + s])
        for s in range(SRC)
    ]
    copies[0].start()
    copies[1].start()
    fields[0].start()
    for copy in copies[2:] + fields[1:]:
        copy.start()

    def tab(name, *args, **kwargs):
        return view(tab_ref, BACKWARD_PLACE, name, *args, **kwargs)

    acc_ref[...] = jnp.zeros_like(acc_ref)
    for copy in copies:
        copy.wait()
    lg = small_ref[0:N, :]
    lg = jnp.concatenate([lg, lg], 0)
    lg = jnp.concatenate([lg, lg], 1)
    block = lane_of((KP, 128)) // 32

    def source(s):
        fields[s].wait()
        row = small_ref[N + s : N + s + 1, :]
        w = picked(row, LANE_WEIGHT)
        a, b = place_of(row, LANE_A, K - KP), place_of(row, LANE_B, K - KP)
        his, los = [], []
        for p in range(C // 2):
            hi, lo = split(fld_ref[s, p] * lg)
            r = dot(tab("d2t"), jnp.concatenate([hi, lo], 0))
            dt = r[:64] + r[64:]
            for h in range(2):
                one = dt[:, 128 * h : 128 * h + 128]
                hi, lo = split(jnp.concatenate([one[:32], one[32:]], 1))
                his.append(hi)
                los.append(lo)
        r = dot(jnp.concatenate(his, 0), tab("g1t"))
        dx = r[:, :128] + r[:, 128:] + dot(
            jnp.concatenate(los, 0), tab("g1t", lanes=slice(0, 128))
        )
        same = jnp.zeros((KP, 128), f32)
        cross = jnp.zeros((KP, 128), f32)
        for c in range(C):
            one = dx[KP * c : KP * c + KP]
            same = same + one * pr_ref[c]
            cross = cross + one * pi_ref[c]
        dwin = same + jnp.where(
            block % 2 == 0, pltpu.roll(cross, 96, 1), pltpu.roll(cross, 32, 1)
        )
        dwin = dwin * (w * (2.0 / (C * SRC)))
        pieces = [jnp.where(block == q, dwin, 0.0) for q in range(4)]
        k0 = pltpu.roll(pieces[0], b, 1) + pltpu.roll(pieces[1], 32 + b, 1)
        k1 = pltpu.roll(pieces[2], 64 + b, 1) + pltpu.roll(pieces[3], 96 + b, 1)
        acc_ref[0, pl.ds(a, KP), :] += k0
        acc_ref[1, pl.ds(a, KP), :] += k1

    for s in range(SRC):
        source(s)
    own = place_of(small_ref[N : N + 1, :], LANE_DEST, SRC - 1)
    loc = loc_ref[own]
    lhi, llo = loc[:, :48], loc[:, 48:96]
    hi, lo = split(jnp.concatenate([acc_ref[0], acc_ref[1]], 1))
    q = dot(lhi, hi) + dot(llo, hi) + dot(lhi, lo)
    both = []
    for k in range(2):
        ks = slice(128 * k, 128 * k + 128)
        both.append(jnp.concatenate([q[:16, ks], q[16:, ks]], 1))
    hi, lo = split(jnp.concatenate(both, 0))
    dm = dot(hi, tab("fin", 0, H)) + dot(hi, tab("fin", H, H)) + dot(lo, tab("fin", 0, H))
    for k in range(2):
        m = mask_ref[0, k]
        out_ref[0, k] = dm[16 * k : 16 * k + 16] - (4.0 * binarize) * m * (1.0 - m * m)


def spec(space=pltpu.VMEM):
    return pl.BlockSpec(memory_space=space)


def limit(mib):
    return pltpu.CompilerParams(vmem_limit_bytes=mib * 1024 * 1024)


def send(masks, weights, shifts):
    return pl.pallas_call(
        send_kernel,
        out_shape=jax.ShapeDtypeStruct((SRC, ROWS, 128), f32),
        in_specs=[spec(), spec(pltpu.SMEM), spec(pltpu.SMEM), spec()],
        out_specs=spec(),
        compiler_params=limit(58),
        name="send",
    )(masks, weights.reshape(1, 1), shifts, jnp.asarray(T["col"]))


def prepare(pupils, labels):
    table = jnp.asarray(FORWARD_TABLE)
    lanes = jax.ShapeDtypeStruct((C, KP, 128), f32)
    return pl.pallas_call(
        prepare_kernel,
        out_shape=(
            lanes, lanes, jax.ShapeDtypeStruct((H, 2 * H), f32),
            jax.ShapeDtypeStruct(table.shape, table.dtype),
        ),
        in_specs=[spec()] * 3,
        out_specs=(spec(),) * 4,
        input_output_aliases={2: 3},
        compiler_params=limit(16),
        name="prepare",
    )(pupils, labels, table)


def forward(gathered, pr, pi, goal, table):
    return pl.pallas_call(
        forward_kernel,
        out_shape=(
            jax.ShapeDtypeStruct((SRC, C // 2, 128, 256), f32),
            jax.ShapeDtypeStruct((N + SRC, 128), f32),
            jax.ShapeDtypeStruct((CLIPS, 128), f32),
        ),
        in_specs=[spec()] * 5,
        out_specs=(spec(), spec(), spec()),
        scratch_shapes=[pltpu.VMEM((2, K, 128), f32), pltpu.VMEM((SRC, N, 128), f32)],
        compiler_params=limit(16),
        name="forward",
    )(gathered, pr, pi, goal, table)


def backward(fld, small, pr, pi, masks):
    table, loc = jnp.asarray(BACKWARD_TABLE), jnp.asarray(T["loc"])
    operands = (fld, small, pr, pi, masks, table, loc)
    return pl.pallas_call(
        backward_kernel,
        out_shape=jax.ShapeDtypeStruct((1, 2, ROWS, H), f32),
        in_specs=[spec(pl.ANY)] * len(operands),
        out_specs=spec(),
        scratch_shapes=[pltpu.VMEM(x.shape, x.dtype) for x in operands]
        + [pltpu.VMEM((2, K, 128), f32), pltpu.SemaphoreType.DMA((len(operands) - 1 + SRC,))],
        compiler_params=limit(58),
        name="backward",
    )(*operands)


def local(gathered, masks, pupils, labels, reduce):
    pr, pi, goal, table = prepare(pupils, labels)
    fld, small, dw = forward(gathered, pr, pi, goal, table)
    parts = reduce(dw)
    return backward(fld, small, pr, pi, masks), parts


def per_device(color_masks, source_weights, pupil_shifts, pupils, target_labels):
    rows = send(color_masks, source_weights, pupil_shifts)
    gathered = lax.all_to_all(rows, "src", 0, 0, tiled=True)
    mask_grad, parts = local(
        gathered, color_masks, pupils, target_labels,
        lambda dw: lax.all_to_all(dw, "clip", 0, 0, tiled=True),
    )
    return mask_grad, jnp.sum(parts)[None]


def solution(mesh):
    in_specs = (P("clip", None, "src", None), P("src"), P("src", None), P(), P("clip", None, None))
    out_specs = (P("clip", None, "src", None), P("src"))
    return jax.shard_map(
        per_device, mesh=mesh, in_specs=in_specs, out_specs=out_specs, check_vma=False
    )
```

```python
import math

import jax
import jax.numpy as jnp
import numpy as np
import ml_dtypes
from jax import lax
from jax.experimental import pallas as pl
from jax.experimental.pallas import tpu as pltpu
from jax.sharding import PartitionSpec as P

H = 256
K = 48
KP = 32
C = 8
SRC = 16
CLIPS = 32
N = 64
ROWS = 16
LATE = 5
EARLY = SRC - LATE

steepness = 4.0
threshold = 0.6
loss_weight = 2.0
binarize = 0.25
f32 = jnp.float32
bf16 = jnp.bfloat16

LANE_WEIGHT, LANE_A, LANE_B, LANE_DEST = 56, 57, 58, 59


def np_split(a):
    a = np.asarray(a, np.float64)
    hi = a.astype(ml_dtypes.bfloat16)
    lo = (a - hi.astype(np.float64)).astype(ml_dtypes.bfloat16)
    return hi, lo


def tables():
    scale = 1.0 / math.sqrt(H * KP)
    x = np.arange(H)
    f = np.arange(K) - K // 2
    ang = 2 * np.pi * ((f[:, None] * x[None, :]) % H) / H
    fc, fs = np.cos(ang) * scale, -np.sin(ang) * scale
    t = {}
    col = np.zeros((2 * H, 128))
    for k in range(2):
        for p in range(25):
            a = 2 * np.pi * ((p * x) % H) / H
            col[k * H : (k + 1) * H, 64 * k + p] = np.cos(a) * scale
            if p:
                col[k * H : (k + 1) * H, 64 * k + 24 + p] = -np.sin(a) * scale
    hi, lo = np_split(col)
    t["col"] = np.concatenate([hi, lo], 1)
    hi, lo = np_split(np.concatenate([fc, fs], 0))
    t["row"] = np.concatenate([hi, lo], 0)
    ex = np.zeros((256, 256))
    for k in range(2):
        for g in range(K):
            p = g - K // 2
            q, s = abs(p), np.sign(p)
            re, im = 128 * k + g, 128 * k + 64 + g
            ex[64 * k + q, re] += 1
            ex[128 + 64 * k + q, im] += 1
            if q:
                ex[128 + 64 * k + 24 + q, re] -= s
                ex[64 * k + 24 + q, im] += s
    t["ex"] = ex.astype(ml_dtypes.bfloat16)
    u = np.arange(N)
    i = np.arange(KP) - KP // 2
    a = 2 * np.pi * ((u[:, None] * i[None, :]) % N) / N
    br, bi = np.cos(a), np.sin(a)
    g1 = np.zeros((128, 256))
    for k in range(2):
        r, m = slice(64 * k, 64 * k + 32), slice(64 * k + 32, 64 * k + 64)
        o, q = slice(64 * k, 64 * k + 64), slice(128 + 64 * k, 128 + 64 * k + 64)
        g1[r, o] = br.T
        g1[m, o] = -bi.T
        g1[r, q] = bi.T
        g1[m, q] = br.T
    hi, lo = np_split(g1)
    t["g1"] = np.concatenate([hi, hi, lo], 0)
    t["g1t"] = np.concatenate([hi.T, lo.T], 1)
    d2 = np.block([[br, -bi], [bi, br]])
    hi, lo = np_split(d2)
    t["d2"] = np.concatenate([hi, hi, lo], 1)
    z = np.zeros_like(lo.T)
    t["d2t"] = np.concatenate(
        [np.concatenate([hi.T, hi.T], 1), np.concatenate([lo.T, z], 1)], 0
    )
    fr = np.arange(-31, 32)
    dx = x[:, None] / H - u[None, :] / N
    up = np.cos(2 * np.pi * fr[:, None, None] * dx[None]).sum(0) / N
    hi, lo = np_split(up)
    t["up"] = np.concatenate([hi, hi, lo], 1)
    t["upt"] = np.concatenate([hi.T, lo.T], 0)
    v = np.zeros((128, 512))
    v[:64, :256] = up.T
    v[64:, 256:] = up.T
    hi, lo = np_split(v)
    t["v"] = np.concatenate([hi, hi, lo], 0)
    t["vt"] = np.concatenate([hi.T, lo.T], 1)
    loc = np.zeros((SRC, 2 * ROWS, K))
    for d in range(SRC):
        sl = slice(ROWS * d, ROWS * d + ROWS)
        loc[d, :ROWS] = fc[:, sl].T
        loc[d, ROWS:] = fs[:, sl].T
    hi, lo = np_split(loc)
    t["loc"] = np.concatenate(
        [hi, lo, np.zeros((SRC, 2 * ROWS, 32), ml_dtypes.bfloat16)], 2
    )
    fin = np.zeros((256, 256))
    fin[0:48] = fc
    fin[64:112] = fs
    fin[128:176] = -fs
    fin[192:240] = fc
    hi, lo = np_split(fin)
    t["fin"] = np.concatenate([hi, lo], 1)
    return t


FORWARD = ("row", "ex", "g1", "d2", "up", "upt", "v", "vt", "d2t", "g1t")
BACKWARD = ("d2t", "g1t", "fin", "g1", "d2")


def pack(t, names):
    parts, place, at = [], {}, 0
    for name in names:
        a = t[name]
        if a.shape[1] == 512:
            a = np.concatenate([a[:, :256], a[:, 256:]], 0)
        a = np.pad(a, ((0, 0), (0, 256 - a.shape[1])))
        parts.append(a)
        place[name] = (at, a.shape[0])
        at += a.shape[0]
    return np.concatenate(parts, 0), place


T = tables()
FORWARD_TABLE, FORWARD_PLACE = pack(T, FORWARD)
BACKWARD_TABLE, BACKWARD_PLACE = pack(T, BACKWARD)


def view(ref, place, name, first=0, count=None, lanes=slice(None)):
    at, rows = place[name]
    return ref[at + first : at + (rows if count is None else first + count), lanes]


def split(x):
    hi = x.astype(bf16)
    lo = (x - hi.astype(f32)).astype(bf16)
    return hi, lo


def dot(a, b):
    return lax.dot_general(
        a, b, (((1,), (0,)), ((), ())), preferred_element_type=f32
    )


def lane_of(shape):
    return lax.broadcasted_iota(jnp.int32, shape, len(shape) - 1)


def send_kernel(mask_ref, weight_ref, shift_ref, col_ref, out_ref):
    m = jnp.concatenate([mask_ref[0, 0], mask_ref[0, 1]], axis=1)
    hi, lo = split(m)
    r = dot(jnp.concatenate([hi, lo], 0), col_ref[...])
    rows = r[:16, :128] + r[16:, :128] + r[:16, 128:]
    lane = lane_of((16, 128))
    rows = jnp.where(lane == LANE_WEIGHT, weight_ref[0, 0], rows)
    rows = jnp.where(lane == LANE_A, shift_ref[0, 0].astype(f32), rows)
    rows = jnp.where(lane == LANE_B, shift_ref[0, 1].astype(f32), rows)
    for d in range(SRC):
        out_ref[d] = jnp.where(lane == LANE_DEST, float(d), rows)


def prepare_kernel(pupil_ref, label_ref, tab_ref, pr_ref, pi_ref, goal_ref, out_ref):
    del tab_ref, out_ref
    sign = jnp.where((lane_of((KP, 128)) // 32) % 2 == 0, -1.0, 1.0)
    for c in range(C):
        re, im = pupil_ref[c, 0], pupil_ref[c, 1]
        pr_ref[c] = jnp.concatenate([re] * 4, axis=1)
        pi_ref[c] = jnp.concatenate([im] * 4, axis=1) * sign
    for k in range(2):
        goal_ref[:, H * k : H * k + H] = (label_ref[0] == k + 1).astype(f32)


def picked(row, which):
    return jnp.sum(jnp.where(lane_of((1, 128)) == which, row, 0.0))


def place_of(row, which, largest):
    return jnp.clip(picked(row, which).astype(jnp.int32), 0, largest)


def source_forward(s, row, spec_ref, pr_ref, pi_ref, tab):
    block = lane_of((KP, 128)) // 32
    a, b = place_of(row, LANE_A, K - KP), place_of(row, LANE_B, K - KP)
    w0 = spec_ref[0, pl.ds(a, KP), :]
    w1 = spec_ref[1, pl.ds(a, KP), :]
    win = jnp.where(
        block < 2,
        jnp.where(block == 0, pltpu.roll(w0, 128 - b, 1), pltpu.roll(w0, 96 - b, 1)),
        jnp.where(block == 2, pltpu.roll(w1, 64 - b, 1), pltpu.roll(w1, 32 - b, 1)),
    )
    swp = jnp.where(block % 2 == 0, pltpu.roll(win, 96, 1), pltpu.roll(win, 32, 1))
    his, los = [], []
    for c in range(C):
        h, l = split(win * pr_ref[c] + swp * pi_ref[c])
        his.append(h)
        los.append(l)
    xhi, xlo = jnp.concatenate(his, 0), jnp.concatenate(los, 0)
    t = dot(jnp.concatenate([xhi, xlo], 1), tab("g1", 0, 256)) + dot(xhi, tab("g1", 256, 128))
    thi, tlo = split(t)
    fields = []
    pw = jnp.zeros((N, 128), f32)
    for p in range(C // 2):
        halves = []
        for c in (2 * p, 2 * p + 1):
            rs = slice(KP * c, KP * c + KP)
            halves.append(
                jnp.concatenate(
                    [thi[rs, :128], thi[rs, 128:], tlo[rs, :128], tlo[rs, 128:],
                     thi[rs, :128], thi[rs, 128:]], 0)
            )
        fld = dot(tab("d2", lanes=slice(0, 192)), jnp.concatenate(halves, 1))
        fields.append(fld)
        q = fld * fld
        q = q[:N] + q[N:]
        pw = pw + (q[:, :128] + q[:, 128:])
    return fields, pw


def source_backward(row, fields, lg, acc_ref, pr_ref, pi_ref, tab):
    block = lane_of((KP, 128)) // 32
    w = picked(row, LANE_WEIGHT)
    a, b = place_of(row, LANE_A, K - KP), place_of(row, LANE_B, K - KP)
    his, los = [], []
    for p in range(C // 2):
        hi, lo = split(fields(p) * lg)
        r = dot(tab("d2t"), jnp.concatenate([hi, lo], 0))
        dt = r[:64] + r[64:]
        for h in range(2):
            one = dt[:, 128 * h : 128 * h + 128]
            hi, lo = split(jnp.concatenate([one[:32], one[32:]], 1))
            his.append(hi)
            los.append(lo)
    r = dot(jnp.concatenate(his, 0), tab("g1t"))
    dx = r[:, :128] + r[:, 128:] + dot(jnp.concatenate(los, 0), tab("g1t", lanes=slice(0, 128)))
    same = jnp.zeros((KP, 128), f32)
    cross = jnp.zeros((KP, 128), f32)
    for c in range(C):
        one = dx[KP * c : KP * c + KP]
        same = same + one * pr_ref[c]
        cross = cross + one * pi_ref[c]
    dwin = same + jnp.where(block % 2 == 0, pltpu.roll(cross, 96, 1), pltpu.roll(cross, 32, 1))
    dwin = dwin * (w * (2.0 / (C * SRC)))
    pieces = [jnp.where(block == q, dwin, 0.0) for q in range(4)]
    k0 = pltpu.roll(pieces[0], b, 1) + pltpu.roll(pieces[1], 32 + b, 1)
    k1 = pltpu.roll(pieces[2], 64 + b, 1) + pltpu.roll(pieces[3], 96 + b, 1)
    acc_ref[0, pl.ds(a, KP), :] += k0
    acc_ref[1, pl.ds(a, KP), :] += k1


def field_weights(lgrad):
    lg = jnp.concatenate([lgrad, lgrad], 0)
    return jnp.concatenate([lg, lg], 1)


def image_kernel(
    g_ref, pr_ref, pi_ref, goal_ref, tab_ref, small_ref, spec_ref, acc_ref, dw_ref,
    fld_ref, pw_ref,
):
    def tab(name, *args, **kwargs):
        return view(tab_ref, FORWARD_PLACE, name, *args, **kwargs)

    g = g_ref[...].reshape(H, 128)
    hi, lo = split(g)
    r = dot(tab("row"), hi)
    u = r[:96] + r[96:] + dot(tab("row", 0, 96), lo)
    uu = jnp.concatenate([u[:48], u[48:]], axis=1)
    hi, lo = split(uu)
    r = dot(jnp.concatenate([hi, lo], 0), tab("ex"))
    r = r[:48] + r[48:]
    spec_ref[0] = r[:, :128]
    spec_ref[1] = r[:, 128:]

    total = jnp.zeros((N, 128), f32)
    for s in range(SRC):
        row = g_ref[s, 0:1, :]
        small_ref[N + s : N + s + 1, :] = row
        fields, pw = source_forward(s, row, spec_ref, pr_ref, pi_ref, tab)
        for p, fld in enumerate(fields):
            if s < EARLY:
                fld_ref[s, p] = fld
        pw_ref[s] = pw
        total = total + picked(row, LANE_WEIGHT) * pw
    hi, lo = split(total * (1.0 / (C * SRC)))
    y = dot(tab("up", lanes=slice(0, 192)), jnp.concatenate([hi, lo, hi], 0))
    hi, lo = split(y)
    both = jnp.concatenate([hi, lo], 1)
    z = jnp.zeros((H, 128), f32)
    for k in range(2):
        intensity = dot(both, tab("v", 384 * k, 256)) + dot(hi, tab("v", 384 * k + 256, 128))
        resist = 1.0 / (1.0 + jnp.exp(-steepness * (intensity - threshold)))
        lg = (resist - goal_ref[:, H * k : H * k + H]) * resist * (1.0 - resist)
        ghi, glo = split((loss_weight * 2.0 * steepness) * lg)
        r = dot(ghi, tab("vt", H * k, H))
        z = z + (r[:, :128] + r[:, 128:] + dot(glo, tab("vt", H * k, H, lanes=slice(0, 128))))
    hi, lo = split(z)
    r = dot(tab("upt"), hi)
    lgrad = r[:N] + r[N:] + dot(tab("upt", 0, N), lo)
    small_ref[0:N, :] = lgrad
    own = place_of(g_ref[0, 0:1, :], LANE_DEST, SRC - 1)
    part = jnp.sum(pw_ref[own] * lgrad, axis=0, keepdims=True)
    part = part * (SRC / (2.0 * CLIPS * H * H) / (C * SRC))
    dw_ref[...] = jnp.broadcast_to(part, (CLIPS, 128))

    acc_ref[...] = jnp.zeros_like(acc_ref)
    lg = field_weights(lgrad)
    for s in range(EARLY):
        source_backward(
            g_ref[s, 0:1, :], lambda p, s=s: fld_ref[s, p], lg, acc_ref, pr_ref, pi_ref, tab
        )


def mask_kernel(
    small_ref, spec_ref, first_ref, pr_ref, pi_ref, mask_ref, tab_ref, loc_ref, out_ref, acc_ref,
):
    def tab(name, *args, **kwargs):
        return view(tab_ref, BACKWARD_PLACE, name, *args, **kwargs)

    acc_ref[...] = first_ref[...]
    lg = field_weights(small_ref[0:N, :])
    for s in range(EARLY, SRC):
        row = small_ref[N + s : N + s + 1, :]
        fields, _ = source_forward(s, row, spec_ref, pr_ref, pi_ref, tab)
        source_backward(row, lambda p, f=fields: f[p], lg, acc_ref, pr_ref, pi_ref, tab)
    own = place_of(small_ref[N : N + 1, :], LANE_DEST, SRC - 1)
    loc = loc_ref[own]
    lhi, llo = loc[:, :48], loc[:, 48:96]
    hi, lo = split(jnp.concatenate([acc_ref[0], acc_ref[1]], 1))
    q = dot(lhi, hi) + dot(llo, hi) + dot(lhi, lo)
    both = []
    for k in range(2):
        ks = slice(128 * k, 128 * k + 128)
        both.append(jnp.concatenate([q[:16, ks], q[16:, ks]], 1))
    hi, lo = split(jnp.concatenate(both, 0))
    dm = dot(hi, tab("fin", 0, H)) + dot(hi, tab("fin", H, H)) + dot(lo, tab("fin", 0, H))
    for k in range(2):
        m = mask_ref[0, k]
        out_ref[0, k] = dm[16 * k : 16 * k + 16] - (4.0 * binarize) * m * (1.0 - m * m)


def spec(space=pltpu.VMEM):
    return pl.BlockSpec(memory_space=space)


def limit(mib):
    return pltpu.CompilerParams(vmem_limit_bytes=mib * 1024 * 1024)


def send(masks, weights, shifts):
    return pl.pallas_call(
        send_kernel,
        out_shape=jax.ShapeDtypeStruct((SRC, ROWS, 128), f32),
        in_specs=[spec(), spec(pltpu.SMEM), spec(pltpu.SMEM), spec()],
        out_specs=spec(),
        compiler_params=limit(58),
        name="send",
    )(masks, weights.reshape(1, 1), shifts, jnp.asarray(T["col"]))


def prepare(pupils, labels):
    table = jnp.asarray(FORWARD_TABLE)
    lanes = jax.ShapeDtypeStruct((C, KP, 128), f32)
    return pl.pallas_call(
        prepare_kernel,
        out_shape=(
            lanes, lanes, jax.ShapeDtypeStruct((H, 2 * H), f32),
            jax.ShapeDtypeStruct(table.shape, table.dtype),
        ),
        in_specs=[spec()] * 3,
        out_specs=(spec(),) * 4,
        input_output_aliases={2: 3},
        compiler_params=limit(16),
        name="prepare",
    )(pupils, labels, table)


def image(gathered, pr, pi, goal, table):
    return pl.pallas_call(
        image_kernel,
        out_shape=(
            jax.ShapeDtypeStruct((N + SRC, 128), f32),
            jax.ShapeDtypeStruct((2, K, 128), f32),
            jax.ShapeDtypeStruct((2, K, 128), f32),
            jax.ShapeDtypeStruct((CLIPS, 128), f32),
        ),
        in_specs=[spec()] * 5,
        out_specs=(spec(),) * 4,
        scratch_shapes=[
            pltpu.VMEM((EARLY, C // 2, 128, 256), f32),
            pltpu.VMEM((SRC, N, 128), f32),
        ],
        compiler_params=limit(24),
        name="image",
    )(gathered, pr, pi, goal, table)


def mask_gradient(small, spectra, first, pr, pi, masks):
    table, loc = jnp.asarray(BACKWARD_TABLE), jnp.asarray(T["loc"])
    operands = (small, spectra, first, pr, pi, masks, table, loc)
    return pl.pallas_call(
        mask_kernel,
        out_shape=jax.ShapeDtypeStruct((1, 2, ROWS, H), f32),
        in_specs=[spec()] * len(operands),
        out_specs=spec(),
        scratch_shapes=[pltpu.VMEM((2, K, 128), f32)],
        compiler_params=limit(16),
        name="mask_gradient",
    )(*operands)


def local(gathered, masks, pupils, labels, reduce):
    pr, pi, goal, table = prepare(pupils, labels)
    small, spectra, first, dw = image(gathered, pr, pi, goal, table)
    parts = reduce(dw)
    return mask_gradient(small, spectra, first, pr, pi, masks), parts


def per_device(color_masks, source_weights, pupil_shifts, pupils, target_labels):
    rows = send(color_masks, source_weights, pupil_shifts)
    gathered = lax.all_to_all(rows, "src", 0, 0, tiled=True)
    mask_grad, parts = local(
        gathered, color_masks, pupils, target_labels,
        lambda dw: lax.all_to_all(dw, "clip", 0, 0, tiled=True),
    )
    return mask_grad, jnp.sum(parts)[None]


def solution(mesh):
    in_specs = (P("clip", None, "src", None), P("src"), P("src", None), P(), P("clip", None, None))
    out_specs = (P("clip", None, "src", None), P("src"))
    return jax.shard_map(
        per_device, mesh=mesh, in_specs=in_specs, out_specs=out_specs, check_vma=False
    )
```

```python
import math

import jax
import jax.numpy as jnp
import numpy as np
import ml_dtypes
from jax import lax
from jax.experimental import pallas as pl
from jax.experimental.pallas import tpu as pltpu
from jax.sharding import PartitionSpec as P

H = 256
K = 48
KP = 32
C = 8
SRC = 16
CLIPS = 32
N = 64
ROWS = 16
LATE = 5
EARLY = SRC - LATE

steepness = 4.0
threshold = 0.6
loss_weight = 2.0
binarize = 0.25
f32 = jnp.float32
bf16 = jnp.bfloat16

SRC_ORDER = [9, 0, 2, 14, 1, 4, 8, 12, 3, 10, 15, 6, 5, 13, 7, 11]
CLIP_ORDER = [18] + [i for i in range(CLIPS) if i != 18]

LANE_WEIGHT, LANE_A, LANE_B, LANE_DEST = 56, 57, 58, 59


def np_split(a):
    a = np.asarray(a, np.float64)
    hi = a.astype(ml_dtypes.bfloat16)
    lo = (a - hi.astype(np.float64)).astype(ml_dtypes.bfloat16)
    return hi, lo


def tables():
    scale = 1.0 / math.sqrt(H * KP)
    x = np.arange(H)
    f = np.arange(K) - K // 2
    ang = 2 * np.pi * ((f[:, None] * x[None, :]) % H) / H
    fc, fs = np.cos(ang) * scale, -np.sin(ang) * scale
    t = {}
    col = np.zeros((2 * H, 128))
    for k in range(2):
        for p in range(25):
            a = 2 * np.pi * ((p * x) % H) / H
            col[k * H : (k + 1) * H, 64 * k + p] = np.cos(a) * scale
            if p:
                col[k * H : (k + 1) * H, 64 * k + 24 + p] = -np.sin(a) * scale
    hi, lo = np_split(col)
    t["col"] = np.concatenate([hi, lo], 1)
    arrival = np.concatenate([np.arange(ROWS * d, ROWS * d + ROWS) for d in SRC_ORDER])
    hi, lo = np_split(np.concatenate([fc, fs], 0)[:, arrival])
    t["row"] = np.concatenate([hi, lo], 0)
    ex = np.zeros((256, 256))
    for k in range(2):
        for g in range(K):
            p = g - K // 2
            q, s = abs(p), np.sign(p)
            re, im = 128 * k + g, 128 * k + 64 + g
            ex[64 * k + q, re] += 1
            ex[128 + 64 * k + q, im] += 1
            if q:
                ex[128 + 64 * k + 24 + q, re] -= s
                ex[64 * k + 24 + q, im] += s
    t["ex"] = ex.astype(ml_dtypes.bfloat16)
    u = np.arange(N)
    i = np.arange(KP) - KP // 2
    a = 2 * np.pi * ((u[:, None] * i[None, :]) % N) / N
    br, bi = np.cos(a), np.sin(a)
    g1 = np.zeros((128, 256))
    for k in range(2):
        r, m = slice(64 * k, 64 * k + 32), slice(64 * k + 32, 64 * k + 64)
        o, q = slice(64 * k, 64 * k + 64), slice(128 + 64 * k, 128 + 64 * k + 64)
        g1[r, o] = br.T
        g1[m, o] = -bi.T
        g1[r, q] = bi.T
        g1[m, q] = br.T
    hi, lo = np_split(g1)
    t["g1"] = np.concatenate([hi, hi, lo], 0)
    t["g1t"] = np.concatenate([hi.T, lo.T], 1)
    d2 = np.block([[br, -bi], [bi, br]])
    hi, lo = np_split(d2)
    t["d2"] = np.concatenate([hi, hi, lo], 1)
    z = np.zeros_like(lo.T)
    t["d2t"] = np.concatenate(
        [np.concatenate([hi.T, hi.T], 1), np.concatenate([lo.T, z], 1)], 0
    )
    fr = np.arange(-31, 32)
    dx = x[:, None] / H - u[None, :] / N
    up = np.cos(2 * np.pi * fr[:, None, None] * dx[None]).sum(0) / N
    hi, lo = np_split(up)
    t["up"] = np.concatenate([hi, hi, lo], 1)
    t["upt"] = np.concatenate([hi.T, lo.T], 0)
    v = np.zeros((128, 512))
    v[:64, :256] = up.T
    v[64:, 256:] = up.T
    hi, lo = np_split(v)
    t["v"] = np.concatenate([hi, hi, lo], 0)
    t["vt"] = np.concatenate([hi.T, lo.T], 1)
    loc = np.zeros((SRC, 2 * ROWS, K))
    for place, d in enumerate(SRC_ORDER):
        sl = slice(ROWS * d, ROWS * d + ROWS)
        loc[place, :ROWS] = fc[:, sl].T
        loc[place, ROWS:] = fs[:, sl].T
    hi, lo = np_split(loc)
    t["loc"] = np.concatenate(
        [hi, lo, np.zeros((SRC, 2 * ROWS, 32), ml_dtypes.bfloat16)], 2
    )
    fin = np.zeros((256, 256))
    fin[0:48] = fc
    fin[64:112] = fs
    fin[128:176] = -fs
    fin[192:240] = fc
    hi, lo = np_split(fin)
    t["fin"] = np.concatenate([hi, lo], 1)
    return t


FORWARD = ("row", "ex", "g1", "d2", "up", "upt", "v", "vt", "d2t", "g1t")
BACKWARD = ("d2t", "g1t", "fin", "g1", "d2")


def pack(t, names):
    parts, place, at = [], {}, 0
    for name in names:
        a = t[name]
        if a.shape[1] == 512:
            a = np.concatenate([a[:, :256], a[:, 256:]], 0)
        a = np.pad(a, ((0, 0), (0, 256 - a.shape[1])))
        parts.append(a)
        place[name] = (at, a.shape[0])
        at += a.shape[0]
    return np.concatenate(parts, 0), place


T = tables()
FORWARD_TABLE, FORWARD_PLACE = pack(T, FORWARD)
BACKWARD_TABLE, BACKWARD_PLACE = pack(T, BACKWARD)


def view(ref, place, name, first=0, count=None, lanes=slice(None)):
    at, rows = place[name]
    return ref[at + first : at + (rows if count is None else first + count), lanes]


def split(x):
    hi = x.astype(bf16)
    lo = (x - hi.astype(f32)).astype(bf16)
    return hi, lo


def dot(a, b):
    return lax.dot_general(
        a, b, (((1,), (0,)), ((), ())), preferred_element_type=f32
    )


def lane_of(shape):
    return lax.broadcasted_iota(jnp.int32, shape, len(shape) - 1)


def send_kernel(mask_ref, weight_ref, shift_ref, col_ref, out_ref):
    m = jnp.concatenate([mask_ref[0, 0], mask_ref[0, 1]], axis=1)
    hi, lo = split(m)
    r = dot(jnp.concatenate([hi, lo], 0), col_ref[...])
    rows = r[:16, :128] + r[16:, :128] + r[:16, 128:]
    lane = lane_of((16, 128))
    rows = jnp.where(lane == LANE_WEIGHT, weight_ref[0, 0], rows)
    rows = jnp.where(lane == LANE_A, shift_ref[0, 0].astype(f32), rows)
    rows = jnp.where(lane == LANE_B, shift_ref[0, 1].astype(f32), rows)
    for d in range(SRC):
        out_ref[d] = jnp.where(lane == LANE_DEST, float(d), rows)


def prepare_kernel(pupil_ref, label_ref, tab_ref, pr_ref, pi_ref, goal_ref, out_ref):
    del tab_ref, out_ref
    sign = jnp.where((lane_of((KP, 128)) // 32) % 2 == 0, -1.0, 1.0)
    for c in range(C):
        re, im = pupil_ref[c, 0], pupil_ref[c, 1]
        pr_ref[c] = jnp.concatenate([re] * 4, axis=1)
        pi_ref[c] = jnp.concatenate([im] * 4, axis=1) * sign
    for k in range(2):
        goal_ref[:, H * k : H * k + H] = (label_ref[0] == k + 1).astype(f32)


def picked(row, which):
    return jnp.sum(jnp.where(lane_of((1, 128)) == which, row, 0.0))


def place_of(row, which, largest):
    return jnp.clip(picked(row, which).astype(jnp.int32), 0, largest)


def source_forward(s, row, spec_ref, pr_ref, pi_ref, tab):
    block = lane_of((KP, 128)) // 32
    a, b = place_of(row, LANE_A, K - KP), place_of(row, LANE_B, K - KP)
    w0 = spec_ref[0, pl.ds(a, KP), :]
    w1 = spec_ref[1, pl.ds(a, KP), :]
    win = jnp.where(
        block < 2,
        jnp.where(block == 0, pltpu.roll(w0, 128 - b, 1), pltpu.roll(w0, 96 - b, 1)),
        jnp.where(block == 2, pltpu.roll(w1, 64 - b, 1), pltpu.roll(w1, 32 - b, 1)),
    )
    swp = jnp.where(block % 2 == 0, pltpu.roll(win, 96, 1), pltpu.roll(win, 32, 1))
    his, los = [], []
    for c in range(C):
        h, l = split(win * pr_ref[c] + swp * pi_ref[c])
        his.append(h)
        los.append(l)
    xhi, xlo = jnp.concatenate(his, 0), jnp.concatenate(los, 0)
    t = dot(jnp.concatenate([xhi, xlo], 1), tab("g1", 0, 256)) + dot(xhi, tab("g1", 256, 128))
    thi, tlo = split(t)
    fields = []
    pw = jnp.zeros((N, 128), f32)
    for p in range(C // 2):
        halves = []
        for c in (2 * p, 2 * p + 1):
            rs = slice(KP * c, KP * c + KP)
            halves.append(
                jnp.concatenate(
                    [thi[rs, :128], thi[rs, 128:], tlo[rs, :128], tlo[rs, 128:],
                     thi[rs, :128], thi[rs, 128:]], 0)
            )
        fld = dot(tab("d2", lanes=slice(0, 192)), jnp.concatenate(halves, 1))
        fields.append(fld)
        q = fld * fld
        q = q[:N] + q[N:]
        pw = pw + (q[:, :128] + q[:, 128:])
    return fields, pw


def source_backward(row, fields, lg, acc_ref, pr_ref, pi_ref, tab):
    block = lane_of((KP, 128)) // 32
    w = picked(row, LANE_WEIGHT)
    a, b = place_of(row, LANE_A, K - KP), place_of(row, LANE_B, K - KP)
    his, los = [], []
    for p in range(C // 2):
        hi, lo = split(fields(p) * lg)
        r = dot(tab("d2t"), jnp.concatenate([hi, lo], 0))
        dt = r[:64] + r[64:]
        for h in range(2):
            one = dt[:, 128 * h : 128 * h + 128]
            hi, lo = split(jnp.concatenate([one[:32], one[32:]], 1))
            his.append(hi)
            los.append(lo)
    r = dot(jnp.concatenate(his, 0), tab("g1t"))
    dx = r[:, :128] + r[:, 128:] + dot(jnp.concatenate(los, 0), tab("g1t", lanes=slice(0, 128)))
    same = jnp.zeros((KP, 128), f32)
    cross = jnp.zeros((KP, 128), f32)
    for c in range(C):
        one = dx[KP * c : KP * c + KP]
        same = same + one * pr_ref[c]
        cross = cross + one * pi_ref[c]
    dwin = same + jnp.where(block % 2 == 0, pltpu.roll(cross, 96, 1), pltpu.roll(cross, 32, 1))
    dwin = dwin * (w * (2.0 / (C * SRC)))
    pieces = [jnp.where(block == q, dwin, 0.0) for q in range(4)]
    k0 = pltpu.roll(pieces[0], b, 1) + pltpu.roll(pieces[1], 32 + b, 1)
    k1 = pltpu.roll(pieces[2], 64 + b, 1) + pltpu.roll(pieces[3], 96 + b, 1)
    acc_ref[0, pl.ds(a, KP), :] += k0
    acc_ref[1, pl.ds(a, KP), :] += k1


def field_weights(lgrad):
    lg = jnp.concatenate([lgrad, lgrad], 0)
    return jnp.concatenate([lg, lg], 1)


def image_kernel(
    g_ref, pr_ref, pi_ref, goal_ref, tab_ref, small_ref, spec_ref, acc_ref, dw_ref,
    fld_ref, pw_ref,
):
    def tab(name, *args, **kwargs):
        return view(tab_ref, FORWARD_PLACE, name, *args, **kwargs)

    g = g_ref[...].reshape(H, 128)
    hi, lo = split(g)
    r = dot(tab("row"), hi)
    u = r[:96] + r[96:] + dot(tab("row", 0, 96), lo)
    uu = jnp.concatenate([u[:48], u[48:]], axis=1)
    hi, lo = split(uu)
    r = dot(jnp.concatenate([hi, lo], 0), tab("ex"))
    r = r[:48] + r[48:]
    spec_ref[0] = r[:, :128]
    spec_ref[1] = r[:, 128:]

    total = jnp.zeros((N, 128), f32)
    for s in range(SRC):
        row = g_ref[s, 0:1, :]
        small_ref[N + s : N + s + 1, :] = row
        fields, pw = source_forward(s, row, spec_ref, pr_ref, pi_ref, tab)
        for p, fld in enumerate(fields):
            if s < EARLY:
                fld_ref[s, p] = fld
        pw_ref[s] = pw
        total = total + picked(row, LANE_WEIGHT) * pw
    hi, lo = split(total * (1.0 / (C * SRC)))
    y = dot(tab("up", lanes=slice(0, 192)), jnp.concatenate([hi, lo, hi], 0))
    hi, lo = split(y)
    both = jnp.concatenate([hi, lo], 1)
    z = jnp.zeros((H, 128), f32)
    for k in range(2):
        intensity = dot(both, tab("v", 384 * k, 256)) + dot(hi, tab("v", 384 * k + 256, 128))
        resist = 1.0 / (1.0 + jnp.exp(-steepness * (intensity - threshold)))
        lg = (resist - goal_ref[:, H * k : H * k + H]) * resist * (1.0 - resist)
        ghi, glo = split((loss_weight * 2.0 * steepness) * lg)
        r = dot(ghi, tab("vt", H * k, H))
        z = z + (r[:, :128] + r[:, 128:] + dot(glo, tab("vt", H * k, H, lanes=slice(0, 128))))
    hi, lo = split(z)
    r = dot(tab("upt"), hi)
    lgrad = r[:N] + r[N:] + dot(tab("upt", 0, N), lo)
    small_ref[0:N, :] = lgrad
    own = place_of(g_ref[0, 0:1, :], LANE_DEST, SRC - 1)
    part = jnp.sum(pw_ref[own] * lgrad, axis=0, keepdims=True)
    part = part * (SRC / (2.0 * CLIPS * H * H) / (C * SRC))
    dw_ref[...] = jnp.broadcast_to(part, (CLIPS, 128))

    acc_ref[...] = jnp.zeros_like(acc_ref)
    lg = field_weights(lgrad)
    for s in range(EARLY):
        source_backward(
            g_ref[s, 0:1, :], lambda p, s=s: fld_ref[s, p], lg, acc_ref, pr_ref, pi_ref, tab
        )


def mask_kernel(
    small_ref, spec_ref, first_ref, pr_ref, pi_ref, mask_ref, tab_ref, loc_ref, out_ref, acc_ref,
):
    def tab(name, *args, **kwargs):
        return view(tab_ref, BACKWARD_PLACE, name, *args, **kwargs)

    acc_ref[...] = first_ref[...]
    lg = field_weights(small_ref[0:N, :])
    for s in range(EARLY, SRC):
        row = small_ref[N + s : N + s + 1, :]
        fields, _ = source_forward(s, row, spec_ref, pr_ref, pi_ref, tab)
        source_backward(row, lambda p, f=fields: f[p], lg, acc_ref, pr_ref, pi_ref, tab)
    own = place_of(small_ref[N : N + 1, :], LANE_DEST, SRC - 1)
    loc = loc_ref[own]
    lhi, llo = loc[:, :48], loc[:, 48:96]
    hi, lo = split(jnp.concatenate([acc_ref[0], acc_ref[1]], 1))
    q = dot(lhi, hi) + dot(llo, hi) + dot(lhi, lo)
    both = []
    for k in range(2):
        ks = slice(128 * k, 128 * k + 128)
        both.append(jnp.concatenate([q[:16, ks], q[16:, ks]], 1))
    hi, lo = split(jnp.concatenate(both, 0))
    dm = dot(hi, tab("fin", 0, H)) + dot(hi, tab("fin", H, H)) + dot(lo, tab("fin", 0, H))
    for k in range(2):
        m = mask_ref[0, k]
        out_ref[0, k] = dm[16 * k : 16 * k + 16] - (4.0 * binarize) * m * (1.0 - m * m)


def spec(space=pltpu.VMEM):
    return pl.BlockSpec(memory_space=space)


def limit(mib):
    return pltpu.CompilerParams(vmem_limit_bytes=mib * 1024 * 1024)


def send(masks, weights, shifts):
    return pl.pallas_call(
        send_kernel,
        out_shape=jax.ShapeDtypeStruct((SRC, ROWS, 128), f32),
        in_specs=[spec(), spec(pltpu.SMEM), spec(pltpu.SMEM), spec()],
        out_specs=spec(),
        compiler_params=limit(58),
        name="send",
    )(masks, weights.reshape(1, 1), shifts, jnp.asarray(T["col"]))


def prepare(pupils, labels):
    table = jnp.asarray(FORWARD_TABLE)
    lanes = jax.ShapeDtypeStruct((C, KP, 128), f32)
    return pl.pallas_call(
        prepare_kernel,
        out_shape=(
            lanes, lanes, jax.ShapeDtypeStruct((H, 2 * H), f32),
            jax.ShapeDtypeStruct(table.shape, table.dtype),
        ),
        in_specs=[spec()] * 3,
        out_specs=(spec(),) * 4,
        input_output_aliases={2: 3},
        compiler_params=limit(16),
        name="prepare",
    )(pupils, labels, table)


def image(gathered, pr, pi, goal, table):
    return pl.pallas_call(
        image_kernel,
        out_shape=(
            jax.ShapeDtypeStruct((N + SRC, 128), f32),
            jax.ShapeDtypeStruct((2, K, 128), f32),
            jax.ShapeDtypeStruct((2, K, 128), f32),
            jax.ShapeDtypeStruct((CLIPS, 128), f32),
        ),
        in_specs=[spec()] * 5,
        out_specs=(spec(),) * 4,
        scratch_shapes=[
            pltpu.VMEM((EARLY, C // 2, 128, 256), f32),
            pltpu.VMEM((SRC, N, 128), f32),
        ],
        compiler_params=limit(24),
        name="image",
    )(gathered, pr, pi, goal, table)


def mask_gradient(small, spectra, first, pr, pi, masks):
    table, loc = jnp.asarray(BACKWARD_TABLE), jnp.asarray(T["loc"])
    operands = (small, spectra, first, pr, pi, masks, table, loc)
    return pl.pallas_call(
        mask_kernel,
        out_shape=jax.ShapeDtypeStruct((1, 2, ROWS, H), f32),
        in_specs=[spec()] * len(operands),
        out_specs=spec(),
        scratch_shapes=[pltpu.VMEM((2, K, 128), f32)],
        compiler_params=limit(16),
        name="mask_gradient",
    )(*operands)


def local(gathered, masks, pupils, labels, reduce):
    pr, pi, goal, table = prepare(pupils, labels)
    small, spectra, first, dw = image(gathered, pr, pi, goal, table)
    parts = reduce(dw)
    return mask_gradient(small, spectra, first, pr, pi, masks), parts


def per_device(color_masks, source_weights, pupil_shifts, pupils, target_labels):
    rows = send(color_masks, source_weights, pupil_shifts)
    gathered = lax.all_to_all(rows, "src", 0, 0, tiled=True, axis_index_groups=[SRC_ORDER])
    mask_grad, parts = local(
        gathered, color_masks, pupils, target_labels,
        lambda dw: lax.all_to_all(
            dw, "clip", 0, 0, tiled=True, axis_index_groups=[CLIP_ORDER]
        ),
    )
    return mask_grad, jnp.sum(parts)[None]


def solution(mesh):
    in_specs = (P("clip", None, "src", None), P("src"), P("src", None), P(), P("clip", None, None))
    out_specs = (P("clip", None, "src", None), P("src"))
    return jax.shard_map(
        per_device, mesh=mesh, in_specs=in_specs, out_specs=out_specs, check_vma=False
    )
```

```python
import math

import jax
import jax.numpy as jnp
import numpy as np
import ml_dtypes
from jax import lax
from jax.experimental import pallas as pl
from jax.experimental.pallas import tpu as pltpu
from jax.sharding import PartitionSpec as P

H = 256
K = 48
KP = 32
C = 8
SRC = 16
CLIPS = 32
N = 64
ROWS = 16
LATE = 8
EARLY = SRC - LATE
FORWARD_GROUP, BACKWARD_GROUP, LATE_GROUP = 4, 4, 4

steepness = 4.0
threshold = 0.6
loss_weight = 2.0
binarize = 0.25
f32 = jnp.float32
bf16 = jnp.bfloat16

SRC_ORDER = [9, 0, 2, 14, 1, 4, 8, 12, 3, 10, 15, 6, 5, 13, 7, 11]
CLIP_ORDER = [18] + [i for i in range(CLIPS) if i != 18]

LANE_WEIGHT, LANE_A, LANE_B, LANE_DEST = 56, 57, 58, 59


def np_split(a):
    a = np.asarray(a, np.float64)
    hi = a.astype(ml_dtypes.bfloat16)
    lo = (a - hi.astype(np.float64)).astype(ml_dtypes.bfloat16)
    return hi, lo


def tables():
    scale = 1.0 / math.sqrt(H * KP)
    x = np.arange(H)
    f = np.arange(K) - K // 2
    ang = 2 * np.pi * ((f[:, None] * x[None, :]) % H) / H
    fc, fs = np.cos(ang) * scale, -np.sin(ang) * scale
    t = {}
    col = np.zeros((2 * H, 128))
    for k in range(2):
        for p in range(25):
            a = 2 * np.pi * ((p * x) % H) / H
            col[k * H : (k + 1) * H, 64 * k + p] = np.cos(a) * scale
            if p:
                col[k * H : (k + 1) * H, 64 * k + 24 + p] = -np.sin(a) * scale
    hi, lo = np_split(col)
    t["col"] = np.concatenate([hi, lo], 1)
    arrival = np.concatenate([np.arange(ROWS * d, ROWS * d + ROWS) for d in SRC_ORDER])
    hi, lo = np_split(np.concatenate([fc, fs], 0)[:, arrival])
    t["row"] = np.concatenate([hi, lo], 0)
    ex = np.zeros((256, 256))
    for k in range(2):
        for g in range(K):
            p = g - K // 2
            q, s = abs(p), np.sign(p)
            re, im = 128 * k + g, 128 * k + 64 + g
            ex[64 * k + q, re] += 1
            ex[128 + 64 * k + q, im] += 1
            if q:
                ex[128 + 64 * k + 24 + q, re] -= s
                ex[64 * k + 24 + q, im] += s
    t["ex"] = ex.astype(ml_dtypes.bfloat16)
    u = np.arange(N)
    i = np.arange(KP) - KP // 2
    a = 2 * np.pi * ((u[:, None] * i[None, :]) % N) / N
    br, bi = np.cos(a), np.sin(a)
    g1 = np.zeros((128, 256))
    for k in range(2):
        r, m = slice(64 * k, 64 * k + 32), slice(64 * k + 32, 64 * k + 64)
        o, q = slice(64 * k, 64 * k + 64), slice(128 + 64 * k, 128 + 64 * k + 64)
        g1[r, o] = br.T
        g1[m, o] = -bi.T
        g1[r, q] = bi.T
        g1[m, q] = br.T
    hi, lo = np_split(g1)
    t["g1"] = np.concatenate([hi, hi, lo], 0)
    t["g1t"] = np.concatenate([hi.T, lo.T], 1)
    d2 = np.block([[br, -bi], [bi, br]])
    hi, lo = np_split(d2)
    t["d2"] = np.concatenate([hi, hi, lo], 1)
    z = np.zeros_like(lo.T)
    t["d2t"] = np.concatenate(
        [np.concatenate([hi.T, hi.T], 1), np.concatenate([lo.T, z], 1)], 0
    )
    fr = np.arange(-31, 32)
    dx = x[:, None] / H - u[None, :] / N
    up = np.cos(2 * np.pi * fr[:, None, None] * dx[None]).sum(0) / N
    hi, lo = np_split(up)
    t["up"] = np.concatenate([hi, hi, lo], 1)
    t["upt"] = np.concatenate([hi.T, lo.T], 0)
    v = np.zeros((128, 512))
    v[:64, :256] = up.T
    v[64:, 256:] = up.T
    hi, lo = np_split(v)
    t["v"] = np.concatenate([hi, hi, lo], 0)
    t["vt"] = np.concatenate([hi.T, lo.T], 1)
    loc = np.zeros((SRC, 2 * ROWS, K))
    for place, d in enumerate(SRC_ORDER):
        sl = slice(ROWS * d, ROWS * d + ROWS)
        loc[place, :ROWS] = fc[:, sl].T
        loc[place, ROWS:] = fs[:, sl].T
    hi, lo = np_split(loc)
    t["loc"] = np.concatenate(
        [hi, lo, np.zeros((SRC, 2 * ROWS, 32), ml_dtypes.bfloat16)], 2
    )
    fin = np.zeros((256, 256))
    fin[0:48] = fc
    fin[64:112] = fs
    fin[128:176] = -fs
    fin[192:240] = fc
    hi, lo = np_split(fin)
    t["fin"] = np.concatenate([hi, lo], 1)
    return t


FORWARD = ("row", "ex", "g1", "d2", "up", "upt", "v", "vt", "d2t", "g1t")
BACKWARD = ("d2t", "g1t", "fin", "g1", "d2")


def pack(t, names):
    parts, place, at = [], {}, 0
    for name in names:
        a = t[name]
        if a.shape[1] == 512:
            a = np.concatenate([a[:, :256], a[:, 256:]], 0)
        a = np.pad(a, ((0, 0), (0, 256 - a.shape[1])))
        parts.append(a)
        place[name] = (at, a.shape[0])
        at += a.shape[0]
    return np.concatenate(parts, 0), place


T = tables()
FORWARD_TABLE, FORWARD_PLACE = pack(T, FORWARD)
BACKWARD_TABLE, BACKWARD_PLACE = pack(T, BACKWARD)


def view(ref, place, name, first=0, count=None, lanes=slice(None)):
    at, rows = place[name]
    return ref[at + first : at + (rows if count is None else first + count), lanes]


def split(x):
    hi = x.astype(bf16)
    lo = (x - hi.astype(f32)).astype(bf16)
    return hi, lo


def dot(a, b):
    return lax.dot_general(
        a, b, (((1,), (0,)), ((), ())), preferred_element_type=f32
    )


def lane_of(shape):
    return lax.broadcasted_iota(jnp.int32, shape, len(shape) - 1)


def send_kernel(mask_ref, weight_ref, shift_ref, col_ref, out_ref):
    m = jnp.concatenate([mask_ref[0, 0], mask_ref[0, 1]], axis=1)
    hi, lo = split(m)
    r = dot(jnp.concatenate([hi, lo], 0), col_ref[...])
    rows = r[:16, :128] + r[16:, :128] + r[:16, 128:]
    lane = lane_of((16, 128))
    rows = jnp.where(lane == LANE_WEIGHT, weight_ref[0, 0], rows)
    rows = jnp.where(lane == LANE_A, shift_ref[0, 0].astype(f32), rows)
    rows = jnp.where(lane == LANE_B, shift_ref[0, 1].astype(f32), rows)
    for d in range(SRC):
        out_ref[d] = jnp.where(lane == LANE_DEST, float(d), rows)


def prepare_kernel(pupil_ref, label_ref, tab_ref, pr_ref, pi_ref, goal_ref, out_ref):
    del tab_ref, out_ref
    sign = jnp.where((lane_of((KP, 128)) // 32) % 2 == 0, -1.0, 1.0)
    for c in range(C):
        re, im = pupil_ref[c, 0], pupil_ref[c, 1]
        pr_ref[c] = jnp.concatenate([re] * 4, axis=1)
        pi_ref[c] = jnp.concatenate([im] * 4, axis=1) * sign
    for k in range(2):
        goal_ref[:, H * k : H * k + H] = (label_ref[0] == k + 1).astype(f32)


def picked(row, which):
    return jnp.sum(jnp.where(lane_of((1, 128)) == which, row, 0.0))


def place_of(row, which, largest):
    return jnp.clip(picked(row, which).astype(jnp.int32), 0, largest)


def sources_forward(rows, spec_ref, pr_ref, pi_ref, tab):
    block = lane_of((KP, 128)) // 32
    his, los = [], []
    for row in rows:
        a, b = place_of(row, LANE_A, K - KP), place_of(row, LANE_B, K - KP)
        w0 = spec_ref[0, pl.ds(a, KP), :]
        w1 = spec_ref[1, pl.ds(a, KP), :]
        win = jnp.where(
            block < 2,
            jnp.where(block == 0, pltpu.roll(w0, 128 - b, 1), pltpu.roll(w0, 96 - b, 1)),
            jnp.where(block == 2, pltpu.roll(w1, 64 - b, 1), pltpu.roll(w1, 32 - b, 1)),
        )
        swp = jnp.where(block % 2 == 0, pltpu.roll(win, 96, 1), pltpu.roll(win, 32, 1))
        for c in range(C):
            h, l = split(win * pr_ref[c] + swp * pi_ref[c])
            his.append(h)
            los.append(l)
    xhi, xlo = jnp.concatenate(his, 0), jnp.concatenate(los, 0)
    t = dot(jnp.concatenate([xhi, xlo], 1), tab("g1", 0, 256)) + dot(xhi, tab("g1", 256, 128))
    thi, tlo = split(t)
    results = []
    for n in range(len(rows)):
        fields = []
        pw = jnp.zeros((N, 128), f32)
        for p in range(C // 2):
            halves = []
            for c in (2 * p, 2 * p + 1):
                at = KP * (C * n + c)
                rs = slice(at, at + KP)
                halves.append(
                    jnp.concatenate(
                        [thi[rs, :128], thi[rs, 128:], tlo[rs, :128], tlo[rs, 128:],
                         thi[rs, :128], thi[rs, 128:]], 0)
                )
            fld = dot(tab("d2", lanes=slice(0, 192)), jnp.concatenate(halves, 1))
            fields.append(fld)
            q = fld * fld
            q = q[:N] + q[N:]
            pw = pw + (q[:, :128] + q[:, 128:])
        results.append((fields, pw))
    return results


def sources_backward(rows, fields, lg, acc_ref, pr_ref, pi_ref, tab):
    block = lane_of((KP, 128)) // 32
    his, los = [], []
    for n in range(len(rows)):
        for p in range(C // 2):
            hi, lo = split(fields(n, p) * lg)
            r = dot(tab("d2t"), jnp.concatenate([hi, lo], 0))
            dt = r[:64] + r[64:]
            for h in range(2):
                one = dt[:, 128 * h : 128 * h + 128]
                hi, lo = split(jnp.concatenate([one[:32], one[32:]], 1))
                his.append(hi)
                los.append(lo)
    r = dot(jnp.concatenate(his, 0), tab("g1t"))
    dx = r[:, :128] + r[:, 128:] + dot(jnp.concatenate(los, 0), tab("g1t", lanes=slice(0, 128)))
    for n, row in enumerate(rows):
        w = picked(row, LANE_WEIGHT)
        a, b = place_of(row, LANE_A, K - KP), place_of(row, LANE_B, K - KP)
        same = jnp.zeros((KP, 128), f32)
        cross = jnp.zeros((KP, 128), f32)
        for c in range(C):
            at = KP * (C * n + c)
            one = dx[at : at + KP]
            same = same + one * pr_ref[c]
            cross = cross + one * pi_ref[c]
        dwin = same + jnp.where(block % 2 == 0, pltpu.roll(cross, 96, 1), pltpu.roll(cross, 32, 1))
        dwin = dwin * (w * (2.0 / (C * SRC)))
        pieces = [jnp.where(block == q, dwin, 0.0) for q in range(4)]
        k0 = pltpu.roll(pieces[0], b, 1) + pltpu.roll(pieces[1], 32 + b, 1)
        k1 = pltpu.roll(pieces[2], 64 + b, 1) + pltpu.roll(pieces[3], 96 + b, 1)
        acc_ref[0, pl.ds(a, KP), :] += k0
        acc_ref[1, pl.ds(a, KP), :] += k1


def groups(first, last, size):
    return [list(range(s, min(s + size, last))) for s in range(first, last, size)]


def field_weights(lgrad):
    lg = jnp.concatenate([lgrad, lgrad], 0)
    return jnp.concatenate([lg, lg], 1)


def image_kernel(
    g_ref, pr_ref, pi_ref, goal_ref, tab_ref, small_ref, spec_ref, acc_ref, dw_ref,
    fld_ref, pw_ref,
):
    def tab(name, *args, **kwargs):
        return view(tab_ref, FORWARD_PLACE, name, *args, **kwargs)

    g = g_ref[...].reshape(H, 128)
    hi, lo = split(g)
    r = dot(tab("row"), hi)
    u = r[:96] + r[96:] + dot(tab("row", 0, 96), lo)
    uu = jnp.concatenate([u[:48], u[48:]], axis=1)
    hi, lo = split(uu)
    r = dot(jnp.concatenate([hi, lo], 0), tab("ex"))
    r = r[:48] + r[48:]
    spec_ref[0] = r[:, :128]
    spec_ref[1] = r[:, 128:]

    total = jnp.zeros((N, 128), f32)
    for group in groups(0, SRC, FORWARD_GROUP):
        rows = [g_ref[s, 0:1, :] for s in group]
        results = sources_forward(rows, spec_ref, pr_ref, pi_ref, tab)
        for s, row, (fields, pw) in zip(group, rows, results):
            small_ref[N + s : N + s + 1, :] = row
            for p, fld in enumerate(fields):
                if s < EARLY:
                    fld_ref[s, p] = fld
            pw_ref[s] = pw
            total = total + picked(row, LANE_WEIGHT) * pw
    hi, lo = split(total * (1.0 / (C * SRC)))
    y = dot(tab("up", lanes=slice(0, 192)), jnp.concatenate([hi, lo, hi], 0))
    hi, lo = split(y)
    both = jnp.concatenate([hi, lo], 1)
    z = jnp.zeros((H, 128), f32)
    for k in range(2):
        intensity = dot(both, tab("v", 384 * k, 256)) + dot(hi, tab("v", 384 * k + 256, 128))
        resist = 1.0 / (1.0 + jnp.exp(-steepness * (intensity - threshold)))
        lg = (resist - goal_ref[:, H * k : H * k + H]) * resist * (1.0 - resist)
        ghi, glo = split((loss_weight * 2.0 * steepness) * lg)
        r = dot(ghi, tab("vt", H * k, H))
        z = z + (r[:, :128] + r[:, 128:] + dot(glo, tab("vt", H * k, H, lanes=slice(0, 128))))
    hi, lo = split(z)
    r = dot(tab("upt"), hi)
    lgrad = r[:N] + r[N:] + dot(tab("upt", 0, N), lo)
    small_ref[0:N, :] = lgrad
    own = place_of(g_ref[0, 0:1, :], LANE_DEST, SRC - 1)
    part = jnp.sum(pw_ref[own] * lgrad, axis=0, keepdims=True)
    part = part * (SRC / (2.0 * CLIPS * H * H) / (C * SRC))
    dw_ref[...] = jnp.broadcast_to(part, (CLIPS, 128))

    acc_ref[...] = jnp.zeros_like(acc_ref)
    lg = field_weights(lgrad)
    for group in groups(0, EARLY, BACKWARD_GROUP):
        sources_backward(
            [g_ref[s, 0:1, :] for s in group], lambda n, p, first=group[0]: fld_ref[first + n, p],
            lg, acc_ref, pr_ref, pi_ref, tab,
        )


def mask_kernel(
    small_ref, spec_ref, first_ref, pr_ref, pi_ref, mask_ref, tab_ref, loc_ref, out_ref, acc_ref,
):
    def tab(name, *args, **kwargs):
        return view(tab_ref, BACKWARD_PLACE, name, *args, **kwargs)

    acc_ref[...] = first_ref[...]
    lg = field_weights(small_ref[0:N, :])
    for group in groups(EARLY, SRC, LATE_GROUP):
        rows = [small_ref[N + s : N + s + 1, :] for s in group]
        results = sources_forward(rows, spec_ref, pr_ref, pi_ref, tab)
        sources_backward(
            rows, lambda n, p, r=results: r[n][0][p], lg, acc_ref, pr_ref, pi_ref, tab
        )
    own = place_of(small_ref[N : N + 1, :], LANE_DEST, SRC - 1)
    loc = loc_ref[own]
    lhi, llo = loc[:, :48], loc[:, 48:96]
    hi, lo = split(jnp.concatenate([acc_ref[0], acc_ref[1]], 1))
    q = dot(lhi, hi) + dot(llo, hi) + dot(lhi, lo)
    both = []
    for k in range(2):
        ks = slice(128 * k, 128 * k + 128)
        both.append(jnp.concatenate([q[:16, ks], q[16:, ks]], 1))
    hi, lo = split(jnp.concatenate(both, 0))
    dm = dot(hi, tab("fin", 0, H)) + dot(hi, tab("fin", H, H)) + dot(lo, tab("fin", 0, H))
    for k in range(2):
        m = mask_ref[0, k]
        out_ref[0, k] = dm[16 * k : 16 * k + 16] - (4.0 * binarize) * m * (1.0 - m * m)


def spec(space=pltpu.VMEM):
    return pl.BlockSpec(memory_space=space)


def limit(mib):
    return pltpu.CompilerParams(vmem_limit_bytes=mib * 1024 * 1024)


def send(masks, weights, shifts):
    return pl.pallas_call(
        send_kernel,
        out_shape=jax.ShapeDtypeStruct((SRC, ROWS, 128), f32),
        in_specs=[spec(), spec(pltpu.SMEM), spec(pltpu.SMEM), spec()],
        out_specs=spec(),
        compiler_params=limit(58),
        name="send",
    )(masks, weights.reshape(1, 1), shifts, jnp.asarray(T["col"]))


def prepare(pupils, labels):
    table = jnp.asarray(FORWARD_TABLE)
    lanes = jax.ShapeDtypeStruct((C, KP, 128), f32)
    return pl.pallas_call(
        prepare_kernel,
        out_shape=(
            lanes, lanes, jax.ShapeDtypeStruct((H, 2 * H), f32),
            jax.ShapeDtypeStruct(table.shape, table.dtype),
        ),
        in_specs=[spec()] * 3,
        out_specs=(spec(),) * 4,
        input_output_aliases={2: 3},
        compiler_params=limit(16),
        name="prepare",
    )(pupils, labels, table)


def image(gathered, pr, pi, goal, table):
    return pl.pallas_call(
        image_kernel,
        out_shape=(
            jax.ShapeDtypeStruct((N + SRC, 128), f32),
            jax.ShapeDtypeStruct((2, K, 128), f32),
            jax.ShapeDtypeStruct((2, K, 128), f32),
            jax.ShapeDtypeStruct((CLIPS, 128), f32),
        ),
        in_specs=[spec()] * 5,
        out_specs=(spec(),) * 4,
        scratch_shapes=[
            pltpu.VMEM((EARLY, C // 2, 128, 256), f32),
            pltpu.VMEM((SRC, N, 128), f32),
        ],
        compiler_params=limit(24),
        name="image",
    )(gathered, pr, pi, goal, table)


def mask_gradient(small, spectra, first, pr, pi, masks):
    table, loc = jnp.asarray(BACKWARD_TABLE), jnp.asarray(T["loc"])
    operands = (small, spectra, first, pr, pi, masks, table, loc)
    return pl.pallas_call(
        mask_kernel,
        out_shape=jax.ShapeDtypeStruct((1, 2, ROWS, H), f32),
        in_specs=[spec()] * len(operands),
        out_specs=spec(),
        scratch_shapes=[pltpu.VMEM((2, K, 128), f32)],
        compiler_params=limit(16),
        name="mask_gradient",
    )(*operands)


def local(gathered, masks, pupils, labels, reduce):
    pr, pi, goal, table = prepare(pupils, labels)
    small, spectra, first, dw = image(gathered, pr, pi, goal, table)
    parts = reduce(dw)
    return mask_gradient(small, spectra, first, pr, pi, masks), parts


def per_device(color_masks, source_weights, pupil_shifts, pupils, target_labels):
    rows = send(color_masks, source_weights, pupil_shifts)
    gathered = lax.all_to_all(rows, "src", 0, 0, tiled=True, axis_index_groups=[SRC_ORDER])
    mask_grad, parts = local(
        gathered, color_masks, pupils, target_labels,
        lambda dw: lax.all_to_all(
            dw, "clip", 0, 0, tiled=True, axis_index_groups=[CLIP_ORDER]
        ),
    )
    return mask_grad, jnp.sum(parts)[None]


def solution(mesh):
    in_specs = (P("clip", None, "src", None), P("src"), P("src", None), P(), P("clip", None, None))
    out_specs = (P("clip", None, "src", None), P("src"))
    return jax.shard_map(
        per_device, mesh=mesh, in_specs=in_specs, out_specs=out_specs, check_vma=False
    )
```

```python
import math

import jax
import jax.numpy as jnp
import numpy as np
import ml_dtypes
from jax import lax
from jax.experimental import pallas as pl
from jax.experimental.pallas import tpu as pltpu
from jax.sharding import PartitionSpec as P

H = 256
K = 48
KP = 32
C = 8
SRC = 16
CLIPS = 32
N = 64
ROWS = 16
LATE = 9
EARLY = SRC - LATE
FORWARD_GROUP, BACKWARD_GROUP, LATE_GROUP = 4, 4, 3

steepness = 4.0
threshold = 0.6
loss_weight = 2.0
binarize = 0.25
f32 = jnp.float32
bf16 = jnp.bfloat16

SRC_ORDER = [9, 0, 2, 14, 1, 4, 8, 12, 3, 10, 15, 6, 5, 13, 7, 11]
CLIP_ORDER = [18] + [i for i in range(CLIPS) if i != 18]

LANE_WEIGHT, LANE_A, LANE_B, LANE_DEST = 56, 57, 58, 59


def np_split(a):
    a = np.asarray(a, np.float64)
    hi = a.astype(ml_dtypes.bfloat16)
    lo = (a - hi.astype(np.float64)).astype(ml_dtypes.bfloat16)
    return hi, lo


def tables():
    scale = 1.0 / math.sqrt(H * KP)
    x = np.arange(H)
    f = np.arange(K) - K // 2
    ang = 2 * np.pi * ((f[:, None] * x[None, :]) % H) / H
    fc, fs = np.cos(ang) * scale, -np.sin(ang) * scale
    t = {}
    col = np.zeros((H, 64))
    for p in range(25):
        a = 2 * np.pi * ((p * x) % H) / H
        col[:, p] = np.cos(a) * scale
        if p:
            col[:, 24 + p] = -np.sin(a) * scale
    t["col"] = np.concatenate(np_split(col), 1)
    arrival = np.concatenate([np.arange(ROWS * d, ROWS * d + ROWS) for d in SRC_ORDER])
    hi, lo = np_split(np.concatenate([fc, fs], 0)[:, arrival])
    t["row"] = np.concatenate([hi, lo], 0)
    ex = np.zeros((256, 256))
    for k in range(2):
        for g in range(K):
            p = g - K // 2
            q, s = abs(p), np.sign(p)
            re, im = 128 * k + g, 128 * k + 64 + g
            ex[64 * k + q, re] += 1
            ex[128 + 64 * k + q, im] += 1
            if q:
                ex[128 + 64 * k + 24 + q, re] -= s
                ex[64 * k + 24 + q, im] += s
    t["ex"] = ex.astype(ml_dtypes.bfloat16)
    u = np.arange(N)
    i = np.arange(KP) - KP // 2
    a = 2 * np.pi * ((u[:, None] * i[None, :]) % N) / N
    br, bi = np.cos(a), np.sin(a)
    g1 = np.zeros((128, 256))
    for k in range(2):
        r, m = slice(64 * k, 64 * k + 32), slice(64 * k + 32, 64 * k + 64)
        o, q = slice(64 * k, 64 * k + 64), slice(128 + 64 * k, 128 + 64 * k + 64)
        g1[r, o] = br.T
        g1[m, o] = -bi.T
        g1[r, q] = bi.T
        g1[m, q] = br.T
    hi, lo = np_split(g1)
    t["g1"] = np.concatenate([hi, hi, lo], 0)
    t["g1t"] = np.concatenate([hi.T, lo.T], 1)
    d2 = np.block([[br, -bi], [bi, br]])
    hi, lo = np_split(d2)
    t["d2"] = np.concatenate([hi, hi, lo], 1)
    z = np.zeros_like(lo.T)
    t["d2t"] = np.concatenate(
        [np.concatenate([hi.T, hi.T], 1), np.concatenate([lo.T, z], 1)], 0
    )
    fr = np.arange(-31, 32)
    dx = x[:, None] / H - u[None, :] / N
    up = np.cos(2 * np.pi * fr[:, None, None] * dx[None]).sum(0) / N
    hi, lo = np_split(up)
    t["up"] = np.concatenate([hi, hi, lo], 1)
    t["upt"] = np.concatenate([hi.T, lo.T], 0)
    v = np.zeros((128, 512))
    v[:64, :256] = up.T
    v[64:, 256:] = up.T
    hi, lo = np_split(v)
    t["v"] = np.concatenate([hi, hi, lo], 0)
    t["vt"] = np.concatenate([hi.T, lo.T], 1)
    loc = np.zeros((SRC, 2 * ROWS, K))
    for place, d in enumerate(SRC_ORDER):
        sl = slice(ROWS * d, ROWS * d + ROWS)
        loc[place, :ROWS] = fc[:, sl].T
        loc[place, ROWS:] = fs[:, sl].T
    hi, lo = np_split(loc)
    t["loc"] = np.concatenate(
        [hi, lo, np.zeros((SRC, 2 * ROWS, 32), ml_dtypes.bfloat16)], 2
    )
    fin = np.zeros((256, 256))
    fin[0:48] = fc
    fin[64:112] = fs
    fin[128:176] = -fs
    fin[192:240] = fc
    hi, lo = np_split(fin)
    t["fin"] = np.concatenate([hi, lo], 1)
    return t


FORWARD = ("row", "ex", "g1", "d2", "up", "upt", "v", "vt", "d2t", "g1t")
BACKWARD = ("d2t", "g1t", "fin", "g1", "d2")


def pack(t, names):
    parts, place, at = [], {}, 0
    for name in names:
        a = t[name]
        if a.shape[1] == 512:
            a = np.concatenate([a[:, :256], a[:, 256:]], 0)
        a = np.pad(a, ((0, 0), (0, 256 - a.shape[1])))
        parts.append(a)
        place[name] = (at, a.shape[0])
        at += a.shape[0]
    return np.concatenate(parts, 0), place


T = tables()
FORWARD_TABLE, FORWARD_PLACE = pack(T, FORWARD)
BACKWARD_TABLE, BACKWARD_PLACE = pack(T, BACKWARD)


def view(ref, place, name, first=0, count=None, lanes=slice(None)):
    at, rows = place[name]
    return ref[at + first : at + (rows if count is None else first + count), lanes]


def split(x):
    hi = x.astype(bf16)
    lo = (x - hi.astype(f32)).astype(bf16)
    return hi, lo


def dot(a, b):
    return lax.dot_general(
        a, b, (((1,), (0,)), ((), ())), preferred_element_type=f32
    )


def lane_of(shape):
    return lax.broadcasted_iota(jnp.int32, shape, len(shape) - 1)


def send_kernel(mask_ref, weight_ref, shift_ref, col_ref, out_ref):
    m = mask_ref[0].reshape(2 * ROWS, H)
    hi, lo = split(m)
    r = dot(jnp.concatenate([hi, lo], 0), col_ref[...])
    r, other = r[:32], r[32:]
    lane = lane_of((ROWS, 128))
    first = r[:16] + other[:16] + pltpu.roll(r[:16], 64, 1)
    second = pltpu.roll(r[16:] + other[16:], 64, 1) + r[16:]
    rows = jnp.where(lane < 64, first, second)
    rows = jnp.where(lane == LANE_WEIGHT, weight_ref[0, 0], rows)
    rows = jnp.where(lane == LANE_A, shift_ref[0, 0].astype(f32), rows)
    rows = jnp.where(lane == LANE_B, shift_ref[0, 1].astype(f32), rows)
    for d in range(SRC):
        out_ref[d] = jnp.where(lane == LANE_DEST, float(d), rows)


def prepare_kernel(pupil_ref, label_ref, tab_ref, pr_ref, pi_ref, goal_ref, out_ref):
    del tab_ref, out_ref
    sign = jnp.where((lane_of((KP, 128)) // 32) % 2 == 0, -1.0, 1.0)
    for c in range(C):
        re, im = pupil_ref[c, 0], pupil_ref[c, 1]
        pr_ref[c] = jnp.concatenate([re] * 4, axis=1)
        pi_ref[c] = jnp.concatenate([im] * 4, axis=1) * sign
    for k in range(2):
        goal_ref[:, H * k : H * k + H] = (label_ref[0] == k + 1).astype(f32)


def picked(row, which):
    return jnp.sum(jnp.where(lane_of((1, 128)) == which, row, 0.0))


def place_of(row, which, largest):
    return jnp.clip(picked(row, which).astype(jnp.int32), 0, largest)


def first_stage(rows, spec_ref, pr_ref, pi_ref, tab):
    block = lane_of((KP, 128)) // 32
    his, los = [], []
    for row in rows:
        a, b = place_of(row, LANE_A, K - KP), place_of(row, LANE_B, K - KP)
        w0 = spec_ref[0, pl.ds(a, KP), :]
        w1 = spec_ref[1, pl.ds(a, KP), :]
        win = jnp.where(
            block < 2,
            jnp.where(block == 0, pltpu.roll(w0, 128 - b, 1), pltpu.roll(w0, 96 - b, 1)),
            jnp.where(block == 2, pltpu.roll(w1, 64 - b, 1), pltpu.roll(w1, 32 - b, 1)),
        )
        swp = jnp.where(block % 2 == 0, pltpu.roll(win, 96, 1), pltpu.roll(win, 32, 1))
        for c in range(C):
            h, l = split(win * pr_ref[c] + swp * pi_ref[c])
            his.append(h)
            los.append(l)
    xhi, xlo = jnp.concatenate(his, 0), jnp.concatenate(los, 0)
    t = dot(jnp.concatenate([xhi, xlo], 1), tab("g1", 0, 256)) + dot(xhi, tab("g1", 256, 128))
    return split(t)


def second_stage(count, pair, tab):
    thi, tlo = pair
    results = []
    for n in range(count):
        fields = []
        pw = jnp.zeros((N, 128), f32)
        for p in range(C // 2):
            halves = []
            for c in (2 * p, 2 * p + 1):
                at = KP * (C * n + c)
                rs = slice(at, at + KP)
                halves.append(
                    jnp.concatenate(
                        [thi[rs, :128], thi[rs, 128:], tlo[rs, :128], tlo[rs, 128:],
                         thi[rs, :128], thi[rs, 128:]], 0)
                )
            fld = dot(tab("d2", lanes=slice(0, 192)), jnp.concatenate(halves, 1))
            fields.append(fld)
            q = fld * fld
            q = q[:N] + q[N:]
            pw = pw + (q[:, :128] + q[:, 128:])
        results.append((fields, pw))
    return results


def sources_backward(rows, fields, lg, acc_ref, pr_ref, pi_ref, tab):
    block = lane_of((KP, 128)) // 32
    his, los = [], []
    for n in range(len(rows)):
        for p in range(C // 2):
            hi, lo = split(fields(n, p) * lg)
            r = dot(tab("d2t"), jnp.concatenate([hi, lo], 0))
            dt = r[:64] + r[64:]
            for h in range(2):
                one = dt[:, 128 * h : 128 * h + 128]
                hi, lo = split(jnp.concatenate([one[:32], one[32:]], 1))
                his.append(hi)
                los.append(lo)
    r = dot(jnp.concatenate(his, 0), tab("g1t"))
    dx = r[:, :128] + r[:, 128:] + dot(jnp.concatenate(los, 0), tab("g1t", lanes=slice(0, 128)))
    for n, row in enumerate(rows):
        w = picked(row, LANE_WEIGHT)
        a, b = place_of(row, LANE_A, K - KP), place_of(row, LANE_B, K - KP)
        same = jnp.zeros((KP, 128), f32)
        cross = jnp.zeros((KP, 128), f32)
        for c in range(C):
            at = KP * (C * n + c)
            one = dx[at : at + KP]
            same = same + one * pr_ref[c]
            cross = cross + one * pi_ref[c]
        dwin = same + jnp.where(block % 2 == 0, pltpu.roll(cross, 96, 1), pltpu.roll(cross, 32, 1))
        dwin = dwin * (w * (2.0 / (C * SRC)))
        pieces = [jnp.where(block == q, dwin, 0.0) for q in range(4)]
        k0 = pltpu.roll(pieces[0], b, 1) + pltpu.roll(pieces[1], 32 + b, 1)
        k1 = pltpu.roll(pieces[2], 64 + b, 1) + pltpu.roll(pieces[3], 96 + b, 1)
        acc_ref[0, pl.ds(a, KP), :] += k0
        acc_ref[1, pl.ds(a, KP), :] += k1


def groups(first, last, size):
    return [list(range(s, min(s + size, last))) for s in range(first, last, size)]


def field_weights(lgrad):
    lg = jnp.concatenate([lgrad, lgrad], 0)
    return jnp.concatenate([lg, lg], 1)


def image_kernel(
    g_ref, pr_ref, pi_ref, goal_ref, tab_ref, small_ref, spec_ref, acc_ref, dw_ref,
    fld_ref, pw_ref,
):
    def tab(name, *args, **kwargs):
        return view(tab_ref, FORWARD_PLACE, name, *args, **kwargs)

    g = g_ref[...].reshape(H, 128)
    hi, lo = split(g)
    r = dot(tab("row"), hi)
    u = r[:96] + r[96:] + dot(tab("row", 0, 96), lo)
    uu = jnp.concatenate([u[:48], u[48:]], axis=1)
    hi, lo = split(uu)
    r = dot(jnp.concatenate([hi, lo], 0), tab("ex"))
    r = r[:48] + r[48:]
    spec_ref[0] = r[:, :128]
    spec_ref[1] = r[:, 128:]

    total = jnp.zeros((N, 128), f32)
    parts = groups(0, SRC, FORWARD_GROUP)

    def first_of(group):
        rows = [g_ref[s, 0:1, :] for s in group]
        return rows, first_stage(rows, spec_ref, pr_ref, pi_ref, tab)

    ahead = first_of(parts[0])
    for i, group in enumerate(parts):
        rows, pair = ahead
        if i + 1 < len(parts):
            ahead = first_of(parts[i + 1])
        results = second_stage(len(group), pair, tab)
        for s, row, (fields, pw) in zip(group, rows, results):
            small_ref[N + s : N + s + 1, :] = row
            for p, fld in enumerate(fields):
                if s < EARLY:
                    fld_ref[s, p] = fld
            pw_ref[s] = pw
            total = total + picked(row, LANE_WEIGHT) * pw
    hi, lo = split(total * (1.0 / (C * SRC)))
    y = dot(tab("up", lanes=slice(0, 192)), jnp.concatenate([hi, lo, hi], 0))
    hi, lo = split(y)
    both = jnp.concatenate([hi, lo], 1)
    z = jnp.zeros((H, 128), f32)
    for k in range(2):
        intensity = dot(both, tab("v", 384 * k, 256)) + dot(hi, tab("v", 384 * k + 256, 128))
        resist = 1.0 / (1.0 + jnp.exp(-steepness * (intensity - threshold)))
        lg = (resist - goal_ref[:, H * k : H * k + H]) * resist * (1.0 - resist)
        ghi, glo = split((loss_weight * 2.0 * steepness) * lg)
        r = dot(ghi, tab("vt", H * k, H))
        z = z + (r[:, :128] + r[:, 128:] + dot(glo, tab("vt", H * k, H, lanes=slice(0, 128))))
    hi, lo = split(z)
    r = dot(tab("upt"), hi)
    lgrad = r[:N] + r[N:] + dot(tab("upt", 0, N), lo)
    small_ref[0:N, :] = lgrad
    own = place_of(g_ref[0, 0:1, :], LANE_DEST, SRC - 1)
    part = jnp.sum(pw_ref[own] * lgrad, axis=0, keepdims=True)
    part = part * (SRC / (2.0 * CLIPS * H * H) / (C * SRC))
    dw_ref[...] = jnp.broadcast_to(part, (CLIPS, 128))

    acc_ref[...] = jnp.zeros_like(acc_ref)
    lg = field_weights(lgrad)
    for group in groups(0, EARLY, BACKWARD_GROUP):
        sources_backward(
            [g_ref[s, 0:1, :] for s in group], lambda n, p, first=group[0]: fld_ref[first + n, p],
            lg, acc_ref, pr_ref, pi_ref, tab,
        )


def mask_kernel(
    small_ref, spec_ref, first_ref, pr_ref, pi_ref, mask_ref, tab_ref, loc_ref, out_ref, acc_ref,
):
    def tab(name, *args, **kwargs):
        return view(tab_ref, BACKWARD_PLACE, name, *args, **kwargs)

    acc_ref[...] = first_ref[...]
    lg = field_weights(small_ref[0:N, :])
    for group in groups(EARLY, SRC, LATE_GROUP):
        rows = [small_ref[N + s : N + s + 1, :] for s in group]
        pair = first_stage(rows, spec_ref, pr_ref, pi_ref, tab)
        results = second_stage(len(rows), pair, tab)
        sources_backward(
            rows, lambda n, p, r=results: r[n][0][p], lg, acc_ref, pr_ref, pi_ref, tab
        )
    own = place_of(small_ref[N : N + 1, :], LANE_DEST, SRC - 1)
    loc = loc_ref[own]
    lhi, llo = loc[:, :48], loc[:, 48:96]
    hi, lo = split(jnp.concatenate([acc_ref[0], acc_ref[1]], 1))
    q = dot(lhi, hi) + dot(llo, hi) + dot(lhi, lo)
    both = []
    for k in range(2):
        ks = slice(128 * k, 128 * k + 128)
        both.append(jnp.concatenate([q[:16, ks], q[16:, ks]], 1))
    hi, lo = split(jnp.concatenate(both, 0))
    dm = dot(hi, tab("fin", 0, H)) + dot(hi, tab("fin", H, H)) + dot(lo, tab("fin", 0, H))
    for k in range(2):
        m = mask_ref[0, k]
        out_ref[0, k] = dm[16 * k : 16 * k + 16] - (4.0 * binarize) * m * (1.0 - m * m)


def spec(space=pltpu.VMEM):
    return pl.BlockSpec(memory_space=space)


def limit(mib):
    return pltpu.CompilerParams(vmem_limit_bytes=mib * 1024 * 1024)


def send(masks, weights, shifts):
    return pl.pallas_call(
        send_kernel,
        out_shape=jax.ShapeDtypeStruct((SRC, ROWS, 128), f32),
        in_specs=[spec(), spec(pltpu.SMEM), spec(pltpu.SMEM), spec()],
        out_specs=spec(),
        compiler_params=limit(58),
        name="send",
    )(masks, weights.reshape(1, 1), shifts, jnp.asarray(T["col"]))


def prepare(pupils, labels):
    table = jnp.asarray(FORWARD_TABLE)
    lanes = jax.ShapeDtypeStruct((C, KP, 128), f32)
    return pl.pallas_call(
        prepare_kernel,
        out_shape=(
            lanes, lanes, jax.ShapeDtypeStruct((H, 2 * H), f32),
            jax.ShapeDtypeStruct(table.shape, table.dtype),
        ),
        in_specs=[spec()] * 3,
        out_specs=(spec(),) * 4,
        input_output_aliases={2: 3},
        compiler_params=limit(16),
        name="prepare",
    )(pupils, labels, table)


def image(gathered, pr, pi, goal, table):
    return pl.pallas_call(
        image_kernel,
        out_shape=(
            jax.ShapeDtypeStruct((N + SRC, 128), f32),
            jax.ShapeDtypeStruct((2, K, 128), f32),
            jax.ShapeDtypeStruct((2, K, 128), f32),
            jax.ShapeDtypeStruct((CLIPS, 128), f32),
        ),
        in_specs=[spec()] * 5,
        out_specs=(spec(),) * 4,
        scratch_shapes=[
            pltpu.VMEM((EARLY, C // 2, 128, 256), f32),
            pltpu.VMEM((SRC, N, 128), f32),
        ],
        compiler_params=limit(24),
        name="image",
    )(gathered, pr, pi, goal, table)


def mask_gradient(small, spectra, first, pr, pi, masks):
    table, loc = jnp.asarray(BACKWARD_TABLE), jnp.asarray(T["loc"])
    operands = (small, spectra, first, pr, pi, masks, table, loc)
    return pl.pallas_call(
        mask_kernel,
        out_shape=jax.ShapeDtypeStruct((1, 2, ROWS, H), f32),
        in_specs=[spec()] * len(operands),
        out_specs=spec(),
        scratch_shapes=[pltpu.VMEM((2, K, 128), f32)],
        compiler_params=limit(16),
        name="mask_gradient",
    )(*operands)


def local(gathered, masks, pupils, labels, reduce):
    pr, pi, goal, table = prepare(pupils, labels)
    small, spectra, first, dw = image(gathered, pr, pi, goal, table)
    parts = reduce(dw)
    return mask_gradient(small, spectra, first, pr, pi, masks), parts


def per_device(color_masks, source_weights, pupil_shifts, pupils, target_labels):
    rows = send(color_masks, source_weights, pupil_shifts)
    gathered = lax.all_to_all(rows, "src", 0, 0, tiled=True, axis_index_groups=[SRC_ORDER])
    mask_grad, parts = local(
        gathered, color_masks, pupils, target_labels,
        lambda dw: lax.all_to_all(
            dw, "clip", 0, 0, tiled=True, axis_index_groups=[CLIP_ORDER]
        ),
    )
    return mask_grad, jnp.sum(parts)[None]


def solution(mesh):
    in_specs = (P("clip", None, "src", None), P("src"), P("src", None), P(), P("clip", None, None))
    out_specs = (P("clip", None, "src", None), P("src"))
    return jax.shard_map(
        per_device, mesh=mesh, in_specs=in_specs, out_specs=out_specs, check_vma=False
    )
```

```python
import math

import jax
import jax.numpy as jnp
import numpy as np
import ml_dtypes
from jax import lax
from jax.experimental import pallas as pl
from jax.experimental.pallas import tpu as pltpu
from jax.sharding import PartitionSpec as P

H = 256
K = 48
KP = 32
C = 8
SRC = 16
CLIPS = 32
N = 64
ROWS = 16
LATE = 12
EARLY = SRC - LATE
FORWARD_GROUP, BACKWARD_GROUP, LATE_GROUP = 4, 4, 4

steepness = 4.0
threshold = 0.6
loss_weight = 2.0
binarize = 0.25
f32 = jnp.float32
bf16 = jnp.bfloat16

SRC_ORDER = [9, 0, 2, 14, 1, 4, 8, 12, 3, 10, 15, 6, 5, 13, 7, 11]
CLIP_ORDER = [18] + [i for i in range(CLIPS) if i != 18]

LANE_WEIGHT, LANE_A, LANE_B, LANE_DEST = 56, 57, 58, 59


def np_split(a):
    a = np.asarray(a, np.float64)
    hi = a.astype(ml_dtypes.bfloat16)
    lo = (a - hi.astype(np.float64)).astype(ml_dtypes.bfloat16)
    return hi, lo


def tables():
    scale = 1.0 / math.sqrt(H * KP)
    x = np.arange(H)
    f = np.arange(K) - K // 2
    ang = 2 * np.pi * ((f[:, None] * x[None, :]) % H) / H
    fc, fs = np.cos(ang) * scale, -np.sin(ang) * scale
    t = {}
    col = np.zeros((H, 64))
    for p in range(25):
        a = 2 * np.pi * ((p * x) % H) / H
        col[:, p] = np.cos(a) * scale
        if p:
            col[:, 24 + p] = -np.sin(a) * scale
    t["col"] = np.concatenate(np_split(col), 1)
    arrival = np.concatenate([np.arange(ROWS * d, ROWS * d + ROWS) for d in SRC_ORDER])
    hi, lo = np_split(np.concatenate([fc, fs], 0)[:, arrival])
    t["row"] = np.concatenate([hi, lo], 0)
    ex = np.zeros((256, 256))
    for k in range(2):
        for g in range(K):
            p = g - K // 2
            q, s = abs(p), np.sign(p)
            re, im = 128 * k + g, 128 * k + 64 + g
            ex[64 * k + q, re] += 1
            ex[128 + 64 * k + q, im] += 1
            if q:
                ex[128 + 64 * k + 24 + q, re] -= s
                ex[64 * k + 24 + q, im] += s
    t["ex"] = ex.astype(ml_dtypes.bfloat16)
    u = np.arange(N)
    i = np.arange(KP) - KP // 2
    a = 2 * np.pi * ((u[:, None] * i[None, :]) % N) / N
    br, bi = np.cos(a), np.sin(a)
    g1 = np.zeros((128, 256))
    for k in range(2):
        r, m = slice(64 * k, 64 * k + 32), slice(64 * k + 32, 64 * k + 64)
        o, q = slice(64 * k, 64 * k + 64), slice(128 + 64 * k, 128 + 64 * k + 64)
        g1[r, o] = br.T
        g1[m, o] = -bi.T
        g1[r, q] = bi.T
        g1[m, q] = br.T
    hi, lo = np_split(g1)
    t["g1"] = np.concatenate([hi, hi, lo], 0)
    t["g1t"] = np.concatenate([hi.T, lo.T], 1)
    d2 = np.block([[br, -bi], [bi, br]])
    hi, lo = np_split(d2)
    t["d2"] = np.concatenate([hi, hi, lo], 1)
    z = np.zeros_like(lo.T)
    t["d2t"] = np.concatenate(
        [np.concatenate([hi.T, hi.T], 1), np.concatenate([lo.T, z], 1)], 0
    )
    fr = np.arange(-31, 32)
    dx = x[:, None] / H - u[None, :] / N
    up = np.cos(2 * np.pi * fr[:, None, None] * dx[None]).sum(0) / N
    hi, lo = np_split(up)
    t["up"] = np.concatenate([hi, hi, lo], 1)
    t["upt"] = np.concatenate([hi.T, lo.T], 0)
    v = np.zeros((128, 512))
    v[:64, :256] = up.T
    v[64:, 256:] = up.T
    hi, lo = np_split(v)
    t["v"] = np.concatenate([hi, hi, lo], 0)
    t["vt"] = np.concatenate([hi.T, lo.T], 1)
    loc = np.zeros((SRC, 2 * ROWS, K))
    for place, d in enumerate(SRC_ORDER):
        sl = slice(ROWS * d, ROWS * d + ROWS)
        loc[place, :ROWS] = fc[:, sl].T
        loc[place, ROWS:] = fs[:, sl].T
    hi, lo = np_split(loc)
    t["loc"] = np.concatenate(
        [hi, lo, np.zeros((SRC, 2 * ROWS, 32), ml_dtypes.bfloat16)], 2
    )
    fin = np.zeros((256, 256))
    fin[0:48] = fc
    fin[64:112] = fs
    fin[128:176] = -fs
    fin[192:240] = fc
    hi, lo = np_split(fin)
    t["fin"] = np.concatenate([hi, lo], 1)
    return t


FORWARD = ("row", "ex", "g1", "d2", "up", "upt", "v", "vt", "d2t", "g1t")
BACKWARD = ("d2t", "g1t", "fin", "g1", "d2")


def pack(t, names):
    parts, place, at = [], {}, 0
    for name in names:
        a = t[name]
        if a.shape[1] == 512:
            a = np.concatenate([a[:, :256], a[:, 256:]], 0)
        a = np.pad(a, ((0, 0), (0, 256 - a.shape[1])))
        parts.append(a)
        place[name] = (at, a.shape[0])
        at += a.shape[0]
    return np.concatenate(parts, 0), place


T = tables()
FORWARD_TABLE, FORWARD_PLACE = pack(T, FORWARD)
BACKWARD_TABLE, BACKWARD_PLACE = pack(T, BACKWARD)


def view(ref, place, name, first=0, count=None, lanes=slice(None)):
    at, rows = place[name]
    return ref[at + first : at + (rows if count is None else first + count), lanes]


def split(x):
    hi = x.astype(bf16)
    lo = (x - hi.astype(f32)).astype(bf16)
    return hi, lo


def dot(a, b):
    return lax.dot_general(
        a, b, (((1,), (0,)), ((), ())), preferred_element_type=f32
    )


def lane_of(shape):
    return lax.broadcasted_iota(jnp.int32, shape, len(shape) - 1)


def send_kernel(mask_ref, weight_ref, shift_ref, col_ref, out_ref):
    m = mask_ref[0].reshape(2 * ROWS, H)
    hi, lo = split(m)
    r = dot(jnp.concatenate([hi, lo], 0), col_ref[...])
    r, other = r[:32], r[32:]
    lane = lane_of((ROWS, 128))
    first = r[:16] + other[:16] + pltpu.roll(r[:16], 64, 1)
    second = pltpu.roll(r[16:] + other[16:], 64, 1) + r[16:]
    rows = jnp.where(lane < 64, first, second)
    rows = jnp.where(lane == LANE_WEIGHT, weight_ref[0, 0], rows)
    rows = jnp.where(lane == LANE_A, shift_ref[0, 0].astype(f32), rows)
    rows = jnp.where(lane == LANE_B, shift_ref[0, 1].astype(f32), rows)
    for d in range(SRC):
        out_ref[d] = jnp.where(lane == LANE_DEST, float(d), rows)


def prepare_kernel(pupil_ref, label_ref, tab_ref, pr_ref, pi_ref, goal_ref, out_ref):
    del tab_ref, out_ref
    sign = jnp.where((lane_of((KP, 128)) // 32) % 2 == 0, -1.0, 1.0)
    for c in range(C):
        re, im = pupil_ref[c, 0], pupil_ref[c, 1]
        pr_ref[c] = jnp.concatenate([re] * 4, axis=1)
        pi_ref[c] = jnp.concatenate([im] * 4, axis=1) * sign
    for k in range(2):
        goal_ref[:, H * k : H * k + H] = (label_ref[0] == k + 1).astype(f32)


def picked(row, which):
    return jnp.sum(jnp.where(lane_of((1, 128)) == which, row, 0.0))


def place_of(row, which, largest):
    return jnp.clip(picked(row, which).astype(jnp.int32), 0, largest)


def first_stage(rows, spec_ref, pr_ref, pi_ref, tab):
    block = lane_of((KP, 128)) // 32
    his, los = [], []
    for row in rows:
        a, b = place_of(row, LANE_A, K - KP), place_of(row, LANE_B, K - KP)
        w0 = spec_ref[0, pl.ds(a, KP), :]
        w1 = spec_ref[1, pl.ds(a, KP), :]
        win = jnp.where(
            block < 2,
            jnp.where(block == 0, pltpu.roll(w0, 128 - b, 1), pltpu.roll(w0, 96 - b, 1)),
            jnp.where(block == 2, pltpu.roll(w1, 64 - b, 1), pltpu.roll(w1, 32 - b, 1)),
        )
        swp = jnp.where(block % 2 == 0, pltpu.roll(win, 96, 1), pltpu.roll(win, 32, 1))
        for c in range(C):
            h, l = split(win * pr_ref[c] + swp * pi_ref[c])
            his.append(h)
            los.append(l)
    xhi, xlo = jnp.concatenate(his, 0), jnp.concatenate(los, 0)
    t = dot(jnp.concatenate([xhi, xlo], 1), tab("g1", 0, 256)) + dot(xhi, tab("g1", 256, 128))
    return split(t)


def second_stage(count, pair, tab):
    thi, tlo = pair
    results = []
    for n in range(count):
        fields = []
        pw = jnp.zeros((N, 128), f32)
        for p in range(C // 2):
            halves = []
            for c in (2 * p, 2 * p + 1):
                at = KP * (C * n + c)
                rs = slice(at, at + KP)
                halves.append(
                    jnp.concatenate(
                        [thi[rs, :128], thi[rs, 128:], tlo[rs, :128], tlo[rs, 128:],
                         thi[rs, :128], thi[rs, 128:]], 0)
                )
            fld = dot(tab("d2", lanes=slice(0, 192)), jnp.concatenate(halves, 1))
            fields.append(fld)
            q = fld * fld
            q = q[:N] + q[N:]
            pw = pw + (q[:, :128] + q[:, 128:])
        results.append((fields, pw))
    return results


def sources_backward(rows, fields, lg, acc_ref, pr_ref, pi_ref, tab):
    block = lane_of((KP, 128)) // 32
    his, los = [], []
    for n in range(len(rows)):
        for p in range(C // 2):
            hi, lo = split(fields(n, p) * lg)
            r = dot(tab("d2t"), jnp.concatenate([hi, lo], 0))
            dt = r[:64] + r[64:]
            for h in range(2):
                one = dt[:, 128 * h : 128 * h + 128]
                hi, lo = split(jnp.concatenate([one[:32], one[32:]], 1))
                his.append(hi)
                los.append(lo)
    r = dot(jnp.concatenate(his, 0), tab("g1t"))
    dx = r[:, :128] + r[:, 128:] + dot(jnp.concatenate(los, 0), tab("g1t", lanes=slice(0, 128)))
    for n, row in enumerate(rows):
        w = picked(row, LANE_WEIGHT)
        a, b = place_of(row, LANE_A, K - KP), place_of(row, LANE_B, K - KP)
        same = jnp.zeros((KP, 128), f32)
        cross = jnp.zeros((KP, 128), f32)
        for c in range(C):
            at = KP * (C * n + c)
            one = dx[at : at + KP]
            same = same + one * pr_ref[c]
            cross = cross + one * pi_ref[c]
        dwin = same + jnp.where(block % 2 == 0, pltpu.roll(cross, 96, 1), pltpu.roll(cross, 32, 1))
        dwin = dwin * (w * (2.0 / (C * SRC)))
        pieces = [jnp.where(block == q, dwin, 0.0) for q in range(4)]
        k0 = pltpu.roll(pieces[0], b, 1) + pltpu.roll(pieces[1], 32 + b, 1)
        k1 = pltpu.roll(pieces[2], 64 + b, 1) + pltpu.roll(pieces[3], 96 + b, 1)
        acc_ref[0, pl.ds(a, KP), :] += k0
        acc_ref[1, pl.ds(a, KP), :] += k1


def groups(first, last, size):
    return [list(range(s, min(s + size, last))) for s in range(first, last, size)]


def field_weights(lgrad):
    lg = jnp.concatenate([lgrad, lgrad], 0)
    return jnp.concatenate([lg, lg], 1)


def image_kernel(
    g_ref, pr_ref, pi_ref, goal_ref, tab_ref, small_ref, spec_ref, acc_ref, dw_ref,
    fld_ref, pw_ref,
):
    def tab(name, *args, **kwargs):
        return view(tab_ref, FORWARD_PLACE, name, *args, **kwargs)

    g = g_ref[...].reshape(H, 128)
    hi, lo = split(g)
    r = dot(tab("row"), hi)
    u = r[:96] + r[96:] + dot(tab("row", 0, 96), lo)
    uu = jnp.concatenate([u[:48], u[48:]], axis=1)
    hi, lo = split(uu)
    r = dot(jnp.concatenate([hi, lo], 0), tab("ex"))
    r = r[:48] + r[48:]
    spec_ref[0] = r[:, :128]
    spec_ref[1] = r[:, 128:]

    total = jnp.zeros((N, 128), f32)
    parts = groups(0, SRC, FORWARD_GROUP)

    def first_of(group):
        rows = [g_ref[s, 0:1, :] for s in group]
        return rows, first_stage(rows, spec_ref, pr_ref, pi_ref, tab)

    ahead = first_of(parts[0])
    for i, group in enumerate(parts):
        rows, pair = ahead
        if i + 1 < len(parts):
            ahead = first_of(parts[i + 1])
        results = second_stage(len(group), pair, tab)
        for s, row, (fields, pw) in zip(group, rows, results):
            small_ref[N + s : N + s + 1, :] = row
            for p, fld in enumerate(fields):
                if s < EARLY:
                    fld_ref[s, p] = fld
            pw_ref[s] = pw
            total = total + picked(row, LANE_WEIGHT) * pw
    hi, lo = split(total * (1.0 / (C * SRC)))
    y = dot(tab("up", lanes=slice(0, 192)), jnp.concatenate([hi, lo, hi], 0))
    hi, lo = split(y)
    both = jnp.concatenate([hi, lo], 1)
    z = jnp.zeros((H, 128), f32)
    for k in range(2):
        intensity = dot(both, tab("v", 384 * k, 256)) + dot(hi, tab("v", 384 * k + 256, 128))
        resist = 1.0 / (1.0 + jnp.exp(-steepness * (intensity - threshold)))
        lg = (resist - goal_ref[:, H * k : H * k + H]) * resist * (1.0 - resist)
        ghi, glo = split((loss_weight * 2.0 * steepness) * lg)
        r = dot(ghi, tab("vt", H * k, H))
        z = z + (r[:, :128] + r[:, 128:] + dot(glo, tab("vt", H * k, H, lanes=slice(0, 128))))
    hi, lo = split(z)
    r = dot(tab("upt"), hi)
    lgrad = r[:N] + r[N:] + dot(tab("upt", 0, N), lo)
    small_ref[0:N, :] = lgrad
    own = place_of(g_ref[0, 0:1, :], LANE_DEST, SRC - 1)
    part = jnp.sum(pw_ref[own] * lgrad, axis=0, keepdims=True)
    part = part * (SRC / (2.0 * CLIPS * H * H) / (C * SRC))
    dw_ref[...] = jnp.broadcast_to(part, (CLIPS, 128))

    acc_ref[...] = jnp.zeros_like(acc_ref)
    lg = field_weights(lgrad)
    for group in groups(0, EARLY, BACKWARD_GROUP):
        sources_backward(
            [g_ref[s, 0:1, :] for s in group], lambda n, p, first=group[0]: fld_ref[first + n, p],
            lg, acc_ref, pr_ref, pi_ref, tab,
        )


def mask_kernel(
    small_ref, spec_ref, first_ref, pr_ref, pi_ref, mask_ref, tab_ref, loc_ref, out_ref, acc_ref,
):
    def tab(name, *args, **kwargs):
        return view(tab_ref, BACKWARD_PLACE, name, *args, **kwargs)

    acc_ref[...] = first_ref[...]
    lg = field_weights(small_ref[0:N, :])
    parts = groups(EARLY, SRC, LATE_GROUP)
    following = {before[0]: after for before, after in zip(parts, parts[1:])}

    def rows_of(group):
        return [small_ref[N + s : N + s + 1, :] for s in group]

    ahead = first_stage(rows_of(parts[0]), spec_ref, pr_ref, pi_ref, tab)
    for group in parts:
        rows = rows_of(group)
        pair = ahead
        if group[-1] + 1 < SRC:
            ahead = first_stage(rows_of(following[group[0]]), spec_ref, pr_ref, pi_ref, tab)
        results = second_stage(len(rows), pair, tab)
        sources_backward(
            rows, lambda n, p, r=results: r[n][0][p], lg, acc_ref, pr_ref, pi_ref, tab
        )
    own = place_of(small_ref[N : N + 1, :], LANE_DEST, SRC - 1)
    loc = loc_ref[own]
    lhi, llo = loc[:, :48], loc[:, 48:96]
    hi, lo = split(jnp.concatenate([acc_ref[0], acc_ref[1]], 1))
    q = dot(lhi, hi) + dot(llo, hi) + dot(lhi, lo)
    both = []
    for k in range(2):
        ks = slice(128 * k, 128 * k + 128)
        both.append(jnp.concatenate([q[:16, ks], q[16:, ks]], 1))
    hi, lo = split(jnp.concatenate(both, 0))
    dm = dot(hi, tab("fin", 0, H)) + dot(hi, tab("fin", H, H)) + dot(lo, tab("fin", 0, H))
    for k in range(2):
        m = mask_ref[0, k]
        out_ref[0, k] = dm[16 * k : 16 * k + 16] - (4.0 * binarize) * m * (1.0 - m * m)


def spec(space=pltpu.VMEM):
    return pl.BlockSpec(memory_space=space)


def limit(mib):
    return pltpu.CompilerParams(vmem_limit_bytes=mib * 1024 * 1024)


def send(masks, weights, shifts):
    return pl.pallas_call(
        send_kernel,
        out_shape=jax.ShapeDtypeStruct((SRC, ROWS, 128), f32),
        in_specs=[spec(), spec(pltpu.SMEM), spec(pltpu.SMEM), spec()],
        out_specs=spec(),
        compiler_params=limit(58),
        name="send",
    )(masks, weights.reshape(1, 1), shifts, jnp.asarray(T["col"]))


def prepare(pupils, labels):
    table = jnp.asarray(FORWARD_TABLE)
    lanes = jax.ShapeDtypeStruct((C, KP, 128), f32)
    return pl.pallas_call(
        prepare_kernel,
        out_shape=(
            lanes, lanes, jax.ShapeDtypeStruct((H, 2 * H), f32),
            jax.ShapeDtypeStruct(table.shape, table.dtype),
        ),
        in_specs=[spec()] * 3,
        out_specs=(spec(),) * 4,
        input_output_aliases={2: 3},
        compiler_params=limit(16),
        name="prepare",
    )(pupils, labels, table)


def image(gathered, pr, pi, goal, table):
    return pl.pallas_call(
        image_kernel,
        out_shape=(
            jax.ShapeDtypeStruct((N + SRC, 128), f32),
            jax.ShapeDtypeStruct((2, K, 128), f32),
            jax.ShapeDtypeStruct((2, K, 128), f32),
            jax.ShapeDtypeStruct((CLIPS, 128), f32),
        ),
        in_specs=[spec()] * 5,
        out_specs=(spec(),) * 4,
        scratch_shapes=[
            pltpu.VMEM((EARLY, C // 2, 128, 256), f32),
            pltpu.VMEM((SRC, N, 128), f32),
        ],
        compiler_params=limit(24),
        name="image",
    )(gathered, pr, pi, goal, table)


def mask_gradient(small, spectra, first, pr, pi, masks):
    table, loc = jnp.asarray(BACKWARD_TABLE), jnp.asarray(T["loc"])
    operands = (small, spectra, first, pr, pi, masks, table, loc)
    return pl.pallas_call(
        mask_kernel,
        out_shape=jax.ShapeDtypeStruct((1, 2, ROWS, H), f32),
        in_specs=[spec()] * len(operands),
        out_specs=spec(),
        scratch_shapes=[pltpu.VMEM((2, K, 128), f32)],
        compiler_params=limit(16),
        name="mask_gradient",
    )(*operands)


def local(gathered, masks, pupils, labels, reduce):
    pr, pi, goal, table = prepare(pupils, labels)
    small, spectra, first, dw = image(gathered, pr, pi, goal, table)
    parts = reduce(dw)
    return mask_gradient(small, spectra, first, pr, pi, masks), parts


def per_device(color_masks, source_weights, pupil_shifts, pupils, target_labels):
    rows = send(color_masks, source_weights, pupil_shifts)
    gathered = lax.all_to_all(rows, "src", 0, 0, tiled=True, axis_index_groups=[SRC_ORDER])
    mask_grad, parts = local(
        gathered, color_masks, pupils, target_labels,
        lambda dw: lax.all_to_all(
            dw, "clip", 0, 0, tiled=True, axis_index_groups=[CLIP_ORDER]
        ),
    )
    return mask_grad, jnp.sum(parts)[None]


def solution(mesh):
    in_specs = (P("clip", None, "src", None), P("src"), P("src", None), P(), P("clip", None, None))
    out_specs = (P("clip", None, "src", None), P("src"))
    return jax.shard_map(
        per_device, mesh=mesh, in_specs=in_specs, out_specs=out_specs, check_vma=False
    )
```
